512 devices in a mesh: layer: 16 (over z, core), col: 32 (over x, y).
Axes of the slice: x: 4, y: 8, z: 8, core: 2. Of those that a mesh axis runs over, the one named last changes fastest.
Arguments:
- factors: bfloat16 [16, 32, 2048, 64], P('layer', 'col'), may hold values from -0.9 to 0.9
- cores: float32 [16, 64, 64], P('layer'), may hold values from -2 to 6, as said below
- tile_list: int32 [256, 2], P('col'), may hold values from 0 to 31, as said below
- probes: bfloat16 [2048, 256, 64], P(None, 'col'), may hold values from -6 to 6
Outputs:
- basis: float32 [2048, 256, 64], P('layer', 'col')
- update_right: float32 [2048, 256, 64], P('layer', 'col')
The draws below stay inside these ranges and needn't reach their ends.
Inputs may be any that keep to these rules, and one draw needn't show every extreme that they name: `tile_list`: each row is a block row and a block column of a tile of the lower triangle: the first is not below the second. `cores`: each matrix is symmetric positive definite: a Gram matrix plus a positive diagonal.
All inputs are finite; a program needn't handle non-finite values.
Results may differ from the reference program's by a relative error of at most 0.02.
Values may be sent and summed in bfloat16 or wider, within the bound.
No kernel may reach another device: no remote copies, remote signals or barrier semaphores. Data moves between devices by JAX's collectives and lax.ppermute only.
A program may use at most 64 MiB of HBM per device.

```python
import math
import jax
import jax.numpy as jnp
from jax import lax

B = 2048
R = 64
PAN_DEV = 1
PANELS = 16
ROWS = 32
NT = 256
N_LAYER = 16


def draw_factors(key, part):
    key_main = jax.random.fold_in(key, 31)
    shape = (PANELS, ROWS, B, R)
    values = jnp.clip(0.15 * jax.random.normal(key_main, shape, jnp.float32), -0.9, 0.9)
    return values.astype(jnp.bfloat16)


def draw_probes(key, part):
    key_main = jax.random.fold_in(key, 41)
    shape = (B, NT, R)
    values = jnp.clip(jax.random.normal(key_main, shape, jnp.float32), -6.0, 6.0)
    return values.astype(jnp.bfloat16)


def draw_cores(key, part):
    key_base = jax.random.fold_in(key, 11)
    key_diag = jax.random.fold_in(key, 12)
    base = jax.random.normal(key_base, (PANELS, R, R), jnp.float32)
    spread = jax.random.uniform(key_diag, (PANELS, R), jnp.float32, 0.5, 2.0)
    gram = jnp.einsum('kab,kcb->kac', base, base) / R
    return gram + spread[:, :, None] * jnp.eye(R, dtype=jnp.float32)[None]


def draw_tile_list(key, part):
    key_one = jax.random.fold_in(key, 21)
    key_two = jax.random.fold_in(key, 22)
    first = jax.random.randint(key_one, (NT,), 0, ROWS)
    second = jax.random.randint(key_two, (NT,), 0, ROWS)
    upper = jnp.maximum(first, second)
    lower = jnp.minimum(first, second)
    upper = upper.at[0].set(ROWS - 1)
    lower = lower.at[0].set(0)
    return jnp.stack([upper, lower], axis=1).astype(jnp.int32)


def setup_inputs(seed: int = 0) -> dict:
    key_of = jax.random.split(jax.random.key(seed), 5)
    return {
        "factors": draw_factors(jax.random.fold_in(key_of[4], 71), 0),
        "cores": draw_cores(jax.random.fold_in(key_of[4], 71), 0),
        "tile_list": draw_tile_list(jax.random.fold_in(key_of[4], 71), 0),
        "probes": draw_probes(jax.random.fold_in(key_of[4], 71), 0),
    }


def reference(factors, cores, tile_list, probes):
    row_first = tile_list[:, 0].astype(jnp.int32)
    row_second = tile_list[:, 1].astype(jnp.int32)
    probe_full = probes.astype(jnp.float32)
    highest = lax.Precision.HIGHEST
    samples = jnp.zeros((B, NT, R), jnp.float32)
    for layer_group in range(N_LAYER):
        block = factors[layer_group * PAN_DEV:(layer_group + 1) * PAN_DEV]
        core_group = cores[layer_group * PAN_DEV:(layer_group + 1) * PAN_DEV]
        left_rows = jnp.take(block, row_first, axis=1).astype(jnp.float32)
        right_rows = jnp.take(block, row_second, axis=1).astype(jnp.float32)
        sketch = jnp.einsum('ktbr,bts->ktrs', right_rows, probe_full)
        core_first = jnp.einsum('kar,ktrs->ktas', core_group, sketch, precision=highest).astype(jnp.bfloat16)
        core_first = lax.optimization_barrier(core_first).astype(jnp.float32)
        part_sample = jnp.einsum('ktbr,ktrs->bts', left_rows, core_first).astype(jnp.bfloat16)
        samples = samples + lax.optimization_barrier(part_sample).astype(jnp.float32)
    gram = jnp.einsum('btr,bts->trs', samples, samples, precision=highest)
    chol = jnp.linalg.cholesky(gram)
    unit_matrix = jnp.broadcast_to(jnp.eye(R, dtype=jnp.float32), chol.shape)
    chol_inverse = jax.scipy.linalg.solve_triangular(chol, unit_matrix, lower=True)
    ortho = jnp.einsum('btr,tsr->bts', samples, chol_inverse, precision=highest)
    ortho_half = ortho.astype(jnp.bfloat16)
    ortho_half = lax.optimization_barrier(ortho_half).astype(jnp.float32)
    update_right = jnp.zeros((B, NT, R), jnp.float32)
    for layer_group in range(N_LAYER):
        block = factors[layer_group * PAN_DEV:(layer_group + 1) * PAN_DEV]
        core_group = cores[layer_group * PAN_DEV:(layer_group + 1) * PAN_DEV]
        left_rows = jnp.take(block, row_first, axis=1).astype(jnp.float32)
        right_rows = jnp.take(block, row_second, axis=1).astype(jnp.float32)
        projected = jnp.einsum('ktbr,bts->ktrs', left_rows, ortho_half)
        core_second = jnp.einsum('kar,ktrs->ktas', core_group, projected, precision=highest).astype(jnp.bfloat16)
        core_second = lax.optimization_barrier(core_second).astype(jnp.float32)
        part_right = jnp.einsum('ktbr,ktrs->bts', right_rows, core_second).astype(jnp.bfloat16)
        update_right = update_right + lax.optimization_barrier(part_right).astype(jnp.float32)
    basis = ortho * math.sqrt(B)
    return (basis, update_right)
```

```python
import math

import jax
import jax.numpy as jnp
from jax import lax
from jax.experimental import pallas as pl
from jax.experimental.pallas import tpu as pltpu
from jax.sharding import Mesh, PartitionSpec as P

F32 = jnp.float32
BF16 = jnp.bfloat16
HIGHEST = lax.Precision.HIGHEST

NZ = 8
NT = 8
RANK = 64
PANELS = 8
DEPTH = PANELS * RANK
ROWS = 256
HALF = 128


def nt_dot(a, b, precision=None):
    return lax.dot_general(
        a, b, (((1,), (1,)), ((), ())), precision=precision, preferred_element_type=F32
    )


def nn_dot(a, b, precision=None):
    return lax.dot_general(
        a, b, (((1,), (0,)), ((), ())), precision=precision, preferred_element_type=F32
    )


def split3(x):
    hi = x.astype(BF16)
    rest = x - hi.astype(F32)
    mid = rest.astype(BF16)
    low = (rest - mid.astype(F32)).astype(BF16)
    return hi, mid, low


def slice_kernel(f_ref, o_ref):
    o_ref[0] = f_ref[...]


def sketch_kernel(rows_ref, z_ref, f_ref, probe_ref, cores_ref, o_ref):
    o_ref[0] = nt_dot(probe_ref[0], f_ref[0]).astype(BF16)


def core_products(total, cores_ref):
    parts = []
    for k in range(PANELS):
        block = total[:, k * RANK:(k + 1) * RANK]
        parts.append(nt_dot(block, cores_ref[k], HIGHEST))
    return parts


def first_kernel(part_ref, cores_ref, o_ref):
    total = part_ref[0].astype(F32)
    for q in range(1, NZ):
        total = total + part_ref[q].astype(F32)
    parts = core_products(total, cores_ref)
    for k in range(PANELS):
        half = parts[k].astype(BF16)
        for q in range(NZ):
            o_ref[q, :, k * RANK:(k + 1) * RANK] = half


def sample_kernel(rows_ref, core_ref, f_ref, o_ref):
    o_ref[0] = nn_dot(core_ref[0], f_ref[0]).astype(BF16)


def gram_kernel(rows_ref, own_ref, other_ref, f_ref, o_ref):
    total = own_ref[0].astype(F32) + other_ref[0].astype(F32)
    gram = nt_dot(total, total, HIGHEST)
    hi = total.astype(BF16)
    low = (total - hi.astype(F32)).astype(BF16)
    both = nt_dot(jnp.concatenate([hi, low], axis=0), f_ref[0])
    o_ref[0, :, 0:DEPTH] = (both[0:RANK] + both[RANK:2 * RANK]).astype(BF16)
    one, two, three = split3(gram)
    o_ref[0, :, DEPTH:DEPTH + RANK] = one
    o_ref[0, :, DEPTH + RANK:DEPTH + 2 * RANK] = two
    o_ref[0, :, DEPTH + 2 * RANK:DEPTH + 3 * RANK] = three
    o_ref[0, :, DEPTH + 3 * RANK:DEPTH + 4 * RANK] = three


def inverse_factor(gram):
    row_id = lax.broadcasted_iota(jnp.int32, (RANK, RANK), 0)
    col_id = lax.broadcasted_iota(jnp.int32, (RANK, RANK), 1)
    unit = jnp.where(row_id == col_id, 1.0, 0.0).astype(F32)
    work = jnp.concatenate([gram, unit], axis=1)
    blocks = [work[8 * b:8 * b + 8, :] for b in range(RANK // 8)]
    sub = lax.broadcasted_iota(jnp.int32, (8, 2 * RANK), 0)
    scales = []
    for p in range(RANK):
        home, at = divmod(p, 8)
        row = blocks[home][at:at + 1, :]
        pivot = row[:, p:p + 1]
        scaled = row * (1.0 / pivot)
        for b in range(home, RANK // 8):
            col = jnp.broadcast_to(blocks[b][:, p:p + 1], (8, 2 * RANK))
            if b == home:
                col = jnp.where(sub > at, col, 0.0)
            blocks[b] = blocks[b] - col * scaled
    work = jnp.concatenate(blocks, axis=0)
    diag = jnp.sum(jnp.where(row_id == col_id, work[:, 0:RANK], 0.0), axis=1, keepdims=True)
    return work[:, RANK:2 * RANK] * (1.0 / jnp.sqrt(diag))


def second_kernel(part_ref, cores_ref, o_ref):
    total = part_ref[0, :, 0:DEPTH].astype(F32)
    for q in range(1, NZ):
        total = total + part_ref[q, :, 0:DEPTH].astype(F32)
    gram = jnp.zeros((RANK, RANK), F32)
    for q in range(NZ):
        one = part_ref[q, :, DEPTH:DEPTH + RANK].astype(F32)
        two = part_ref[q, :, DEPTH + RANK:DEPTH + 2 * RANK].astype(F32)
        three = part_ref[q, :, DEPTH + 2 * RANK:DEPTH + 3 * RANK].astype(F32)
        gram = gram + (one + (two + three))
    inverse = inverse_factor(gram)
    projected = nn_dot(inverse, total, HIGHEST)
    parts = core_products(projected, cores_ref)
    one, two, _ = split3(inverse)
    for q in range(NZ):
        for k in range(PANELS):
            o_ref[q, :, k * RANK:(k + 1) * RANK] = parts[k].astype(BF16)
        o_ref[q, :, DEPTH:DEPTH + RANK] = one
        o_ref[q, :, DEPTH + RANK:DEPTH + 2 * RANK] = two


def final_kernel(rows_ref, side_ref, core_ref, own_ref, other_ref, f_ref, basis_ref, keep_ref, send_ref):
    inverse = core_ref[0, :, DEPTH:DEPTH + RANK].astype(F32)
    inverse = inverse + core_ref[0, :, DEPTH + RANK:DEPTH + 2 * RANK].astype(F32)
    total = own_ref[0].astype(F32) + other_ref[0].astype(F32)
    basis_ref[0] = nn_dot(inverse, total, HIGHEST) * math.sqrt(2048.0)
    part = nn_dot(core_ref[0, :, 0:DEPTH], f_ref[0])
    first, last = part[:, 0:HALF], part[:, HALF:ROWS]
    upper = side_ref[0] == 1
    keep_ref[0] = jnp.where(upper, last, first)
    send_ref[0] = jnp.where(upper, first, last).astype(BF16)


def in_hbm(x):
    return pltpu.with_memory_space_constraint(x, pltpu.HBM)


def local(factors, cores, tile_list, probes):
    swap = [(0, 1), (1, 0)]
    z = lax.axis_index("z").astype(jnp.int32).reshape(1)
    side = lax.axis_index("core").astype(jnp.int32).reshape(1)
    row_first = tile_list[:, 0].astype(jnp.int32)
    row_second = tile_list[:, 1].astype(jnp.int32)
    params = pltpu.CompilerParams(vmem_limit_bytes=32 * 1024 * 1024)

    def call(kernel, scalars, out_shape, in_specs, out_specs, *args):
        return pl.pallas_call(
            kernel,
            out_shape=out_shape,
            grid_spec=pltpu.PrefetchScalarGridSpec(
                num_scalar_prefetch=len(scalars), grid=(NT,), in_specs=in_specs, out_specs=out_specs
            ),
            compiler_params=params,
        )(*scalars, *args)

    def tile_spec(rows, lanes):
        return pl.BlockSpec((1, rows, lanes), lambda t, *_: (t, 0, 0))

    gathered_spec = pl.BlockSpec((1, DEPTH, ROWS), lambda t, rows, *_: (rows[t], 0, 0))

    def exchange(x):
        return lax.all_to_all(x, "z", 0, 0, tiled=True)

    mine = jnp.transpose(factors[0, 0], (1, 0))
    sliced = call(
        slice_kernel,
        (),
        jax.ShapeDtypeStruct((NZ, RANK, ROWS), BF16),
        [pl.BlockSpec((RANK, ROWS), lambda t: (0, t))],
        pl.BlockSpec((1, RANK, ROWS), lambda t: (t, 0, 0)),
        mine,
    )
    panels = exchange(sliced).reshape(DEPTH, ROWS)
    gathered = in_hbm(lax.all_gather(panels, ("x", "y"), axis=0, tiled=False))
    core, _ = lax.optimization_barrier((cores[0], panels))
    all_cores = lax.all_gather(core, "z", axis=0, tiled=False)

    probe = in_hbm(jnp.transpose(probes, (1, 2, 0)))
    sketch = call(
        sketch_kernel,
        (row_second, z),
        jax.ShapeDtypeStruct((NT, RANK, DEPTH), BF16),
        [
            gathered_spec,
            pl.BlockSpec((1, RANK, ROWS), lambda t, rows, zz: (t, 0, zz[0])),
            pl.BlockSpec(memory_space=pl.ANY),
        ],
        tile_spec(RANK, DEPTH),
        gathered,
        probe,
        all_cores,
    )
    sketch = exchange(sketch)
    first = pl.pallas_call(
        first_kernel, out_shape=jax.ShapeDtypeStruct((NZ, RANK, DEPTH), BF16), compiler_params=params
    )(sketch, all_cores)
    first = exchange(first)
    own = call(
        sample_kernel,
        (row_first,),
        jax.ShapeDtypeStruct((NT, RANK, ROWS), BF16),
        [tile_spec(RANK, DEPTH), gathered_spec],
        tile_spec(RANK, ROWS),
        first,
        gathered,
    )
    other = lax.ppermute(own, "core", swap)
    wide = DEPTH + 4 * RANK
    stacked = call(
        gram_kernel,
        (row_first,),
        jax.ShapeDtypeStruct((NT, RANK, wide), BF16),
        [tile_spec(RANK, ROWS), tile_spec(RANK, ROWS), gathered_spec],
        tile_spec(RANK, wide),
        own,
        other,
        gathered,
    )
    stacked = exchange(stacked)
    wide = DEPTH + 2 * RANK
    second = pl.pallas_call(
        second_kernel, out_shape=jax.ShapeDtypeStruct((NZ, RANK, wide), BF16), compiler_params=params
    )(stacked, all_cores)
    second = exchange(second)
    half_spec = pl.BlockSpec((1, RANK, HALF), lambda t, rows, ss: (t, 0, ss[0]))
    basis, keep, send = call(
        final_kernel,
        (row_second, side),
        (
            jax.ShapeDtypeStruct((NT, RANK, HALF), F32),
            jax.ShapeDtypeStruct((NT, RANK, HALF), F32),
            jax.ShapeDtypeStruct((NT, RANK, HALF), BF16),
        ),
        [tile_spec(RANK, wide), half_spec, half_spec, gathered_spec],
        (tile_spec(RANK, HALF), tile_spec(RANK, HALF), tile_spec(RANK, HALF)),
        second,
        own,
        other,
        gathered,
    )
    update = keep + lax.ppermute(send, "core", swap).astype(F32)
    return jnp.transpose(basis, (2, 0, 1)), jnp.transpose(update, (2, 0, 1))


def solution(mesh):
    fine = Mesh(mesh.devices.reshape(8, 2, 4, 8), ("z", "core", "x", "y"))
    layer, col = ("z", "core"), ("x", "y")
    placed = (
        P(layer, col, None, None),
        P(layer, None, None),
        P(col, None),
        P(None, col, None),
    )
    return jax.shard_map(
        local,
        mesh=fine,
        in_specs=placed,
        out_specs=(P(layer, col, None), P(layer, col, None)),
        check_vma=False,
    )
```

```python
import math

import jax
import jax.numpy as jnp
from jax import lax
from jax.experimental import pallas as pl
from jax.experimental.pallas import tpu as pltpu
from jax.sharding import Mesh, PartitionSpec as P

F32 = jnp.float32
BF16 = jnp.bfloat16
HIGHEST = lax.Precision.HIGHEST

NZ = 8
NT = 8
RANK = 64
PANELS = 8
DEPTH = PANELS * RANK
ROWS = 256
HALF = 128


def nt_dot(a, b, precision=None):
    return lax.dot_general(
        a, b, (((1,), (1,)), ((), ())), precision=precision, preferred_element_type=F32
    )


def nn_dot(a, b, precision=None):
    return lax.dot_general(
        a, b, (((1,), (0,)), ((), ())), precision=precision, preferred_element_type=F32
    )


def split3(x):
    hi = x.astype(BF16)
    rest = x - hi.astype(F32)
    mid = rest.astype(BF16)
    low = (rest - mid.astype(F32)).astype(BF16)
    return hi, mid, low


def slice_kernel(f_ref, o_ref):
    o_ref[0] = f_ref[...]


def sketch_kernel(first_ref, second_ref, z_ref, f_ref, probe_ref, cores_ref, o_ref, left_ref, right_ref,
                  slot_ref, sem_right, sem_left, sem_probe):
    start = pl.multiple_of(z_ref[0] * ROWS, ROWS)
    rights, probes, lefts = [], [], []
    for t in range(NT):
        rights.append(pltpu.make_async_copy(f_ref.at[second_ref[t]], right_ref.at[t], sem_right.at[t]))
        probes.append(
            pltpu.make_async_copy(probe_ref.at[t, :, pl.ds(start, ROWS)], slot_ref.at[t], sem_probe.at[t])
        )
        lefts.append(pltpu.make_async_copy(f_ref.at[first_ref[t]], left_ref.at[t], sem_left.at[t]))
    for t in range(NT):
        rights[t].start()
        probes[t].start()
    for t in range(NT):
        lefts[t].start()
    for t in range(NT):
        rights[t].wait()
        probes[t].wait()
        o_ref[t] = nt_dot(slot_ref[t], right_ref[t]).astype(BF16)
    for t in range(NT):
        lefts[t].wait()


def core_products(total, cores_ref):
    parts = []
    for k in range(PANELS):
        block = total[:, k * RANK:(k + 1) * RANK]
        parts.append(nt_dot(block, cores_ref[k], HIGHEST))
    return parts


def first_kernel(part_ref, cores_ref, o_ref):
    total = part_ref[0].astype(F32)
    for q in range(1, NZ):
        total = total + part_ref[q].astype(F32)
    parts = core_products(total, cores_ref)
    for k in range(PANELS):
        half = parts[k].astype(BF16)
        for q in range(NZ):
            o_ref[q, :, k * RANK:(k + 1) * RANK] = half


def sample_kernel(core_ref, f_ref, o_ref):
    for t in range(NT):
        o_ref[t] = nn_dot(core_ref[t], f_ref[t]).astype(BF16)


def pack_gram(gram):
    row = lax.broadcasted_iota(jnp.int32, (RANK, RANK), 0)
    col = lax.broadcasted_iota(jnp.int32, (RANK, RANK), 1)
    one, two, three = (part.astype(F32) for part in split3(gram))
    diag = jnp.sum(jnp.where(row == col, two, 0.0), axis=1, keepdims=True)
    last = jnp.sum(jnp.where((row == RANK - 1) & (col == RANK - 1), two, 0.0), axis=(0, 1), keepdims=True)
    upper = jnp.where(col == row + 1, diag, 0.0)
    upper = jnp.where((row == 0) & (col == RANK - 1), last, upper)
    return jnp.where(col <= row, one, jnp.transpose(two)), jnp.where(col <= row, three, upper)


def unpack_gram(left, right):
    row = lax.broadcasted_iota(jnp.int32, (RANK, RANK), 0)
    col = lax.broadcasted_iota(jnp.int32, (RANK, RANK), 1)
    corner = (row == 0) & (col == RANK - 1)
    last = jnp.sum(jnp.where(corner, right, 0.0), axis=(0, 1), keepdims=True)
    diag = jnp.sum(jnp.where(col == row + 1, right, 0.0), axis=1, keepdims=True)
    two_diag = jnp.where((row == col) & (row < RANK - 1), diag, 0.0)
    two_diag = jnp.where((row == RANK - 1) & (col == RANK - 1), last, two_diag)
    lower = col <= row
    one = jnp.where(lower, left, 0.0)
    three = jnp.where(lower, right, 0.0)
    two = jnp.where(col > row, left, 0.0)
    strict = jnp.where(col < row, one, 0.0) + jnp.where(col < row, three, 0.0)
    full_diag = jnp.where(row == col, one + (three + two_diag), 0.0)
    below = strict + jnp.where(col < row, jnp.transpose(two), 0.0)
    return below + full_diag + jnp.transpose(below)


def gram_kernel(own_ref, other_ref, f_ref, o_ref):
    for t in range(NT):
        total = own_ref[t].astype(F32) + other_ref[t].astype(F32)
        gram = nt_dot(total, total, HIGHEST)
        hi = total.astype(BF16)
        low = (total - hi.astype(F32)).astype(BF16)
        both = nt_dot(jnp.concatenate([hi, low], axis=0), f_ref[t])
        o_ref[t, :, 0:DEPTH] = (both[0:RANK] + both[RANK:2 * RANK]).astype(BF16)
        left, right = pack_gram(gram)
        o_ref[t, :, DEPTH:DEPTH + 2 * RANK] = jnp.concatenate([left, right], axis=1).astype(BF16)


def inverse_factor(gram):
    row_id = lax.broadcasted_iota(jnp.int32, (RANK, RANK), 0)
    col_id = lax.broadcasted_iota(jnp.int32, (RANK, RANK), 1)
    unit = jnp.where(row_id == col_id, 1.0, 0.0).astype(F32)
    work = jnp.concatenate([gram, unit], axis=1)
    blocks = [work[8 * b:8 * b + 8, :] for b in range(RANK // 8)]
    sub = lax.broadcasted_iota(jnp.int32, (8, 2 * RANK), 0)
    scales = []
    for p in range(RANK):
        home, at = divmod(p, 8)
        row = blocks[home][at:at + 1, :]
        pivot = row[:, p:p + 1]
        scaled = row * (1.0 / pivot)
        for b in range(home, RANK // 8):
            col = jnp.broadcast_to(blocks[b][:, p:p + 1], (8, 2 * RANK))
            if b == home:
                col = jnp.where(sub > at, col, 0.0)
            blocks[b] = blocks[b] - col * scaled
    work = jnp.concatenate(blocks, axis=0)
    diag = jnp.sum(jnp.where(row_id == col_id, work[:, 0:RANK], 0.0), axis=1, keepdims=True)
    return work[:, RANK:2 * RANK] * (1.0 / jnp.sqrt(diag))


def second_kernel(part_ref, cores_ref, o_ref):
    total = part_ref[0, :, 0:DEPTH].astype(F32)
    for q in range(1, NZ):
        total = total + part_ref[q, :, 0:DEPTH].astype(F32)
    packed = part_ref[0, :, DEPTH:DEPTH + 2 * RANK].astype(F32)
    for q in range(1, NZ):
        packed = packed + part_ref[q, :, DEPTH:DEPTH + 2 * RANK].astype(F32)
    gram = unpack_gram(packed[:, 0:RANK], packed[:, RANK:2 * RANK])
    inverse = inverse_factor(gram)
    projected = nn_dot(inverse, total, HIGHEST)
    parts = core_products(projected, cores_ref)
    one, two, _ = split3(inverse)
    for q in range(NZ):
        for k in range(PANELS):
            o_ref[q, :, k * RANK:(k + 1) * RANK] = parts[k].astype(BF16)
        o_ref[q, :, DEPTH:DEPTH + RANK] = one
        o_ref[q, :, DEPTH + RANK:DEPTH + 2 * RANK] = two


def final_kernel(side_ref, core_ref, own_ref, other_ref, f_ref, basis_ref, keep_ref, send_ref):
    upper = side_ref[0] == 1
    for t in range(NT):
        inverse = core_ref[t, :, DEPTH:DEPTH + RANK].astype(F32)
        inverse = inverse + core_ref[t, :, DEPTH + RANK:DEPTH + 2 * RANK].astype(F32)
        total = own_ref[t].astype(F32) + other_ref[t].astype(F32)
        half = jnp.where(upper, total[:, HALF:ROWS], total[:, 0:HALF])
        basis_ref[t] = nn_dot(inverse, half, HIGHEST) * math.sqrt(2048.0)
        part = nn_dot(core_ref[t, :, 0:DEPTH], f_ref[t])
        first, last = part[:, 0:HALF], part[:, HALF:ROWS]
        keep_ref[t] = jnp.where(upper, last, first)
        send_ref[t] = jnp.where(upper, first, last).astype(BF16)


def in_hbm(x):
    return pltpu.with_memory_space_constraint(x, pltpu.HBM)


def local(factors, cores, tile_list, probes):
    swap = [(0, 1), (1, 0)]
    z = lax.axis_index("z").astype(jnp.int32).reshape(1)
    side = lax.axis_index("core").astype(jnp.int32).reshape(1)
    row_first = tile_list[:, 0].astype(jnp.int32)
    row_second = tile_list[:, 1].astype(jnp.int32)
    params = pltpu.CompilerParams(vmem_limit_bytes=32 * 1024 * 1024)

    smem = pl.BlockSpec(memory_space=pltpu.SMEM)
    hbm = pl.BlockSpec(memory_space=pl.ANY)
    vmem = pl.BlockSpec(memory_space=pltpu.VMEM)

    def call(kernel, out_shape, in_specs, *args, scratch=()):
        return pl.pallas_call(
            kernel,
            out_shape=out_shape,
            in_specs=in_specs,
            out_specs=jax.tree.map(lambda _: vmem, out_shape),
            scratch_shapes=scratch,
            compiler_params=params,
        )(*args)

    def shape(*dims, dtype=BF16):
        return jax.ShapeDtypeStruct(dims, dtype)

    def exchange(x):
        return lax.all_to_all(x, "z", 0, 0, tiled=True)

    mine = jnp.transpose(factors[0, 0], (1, 0))
    sliced = pl.pallas_call(
        slice_kernel,
        out_shape=shape(NZ, RANK, ROWS),
        grid=(NZ,),
        in_specs=[pl.BlockSpec((RANK, ROWS), lambda t: (0, t))],
        out_specs=pl.BlockSpec((1, RANK, ROWS), lambda t: (t, 0, 0)),
        compiler_params=params,
    )(mine)
    panels = exchange(sliced).reshape(DEPTH, ROWS)
    gathered = in_hbm(lax.all_gather(panels, ("x", "y"), axis=0, tiled=False))
    core, _ = lax.optimization_barrier((cores[0], panels))
    all_cores = lax.all_gather(core, "z", axis=0, tiled=False)

    probe = in_hbm(jnp.transpose(probes, (1, 2, 0)))
    block = shape(NT, DEPTH, ROWS)
    sketch, left, right = call(
        sketch_kernel,
        (shape(NT, RANK, DEPTH), block, block),
        [smem, smem, smem, hbm, hbm, hbm],
        row_first,
        row_second,
        z,
        gathered,
        probe,
        all_cores,
        scratch=[pltpu.VMEM((NT, RANK, ROWS), BF16)] + [pltpu.SemaphoreType.DMA((NT,))] * 3,
    )
    first = call(first_kernel, shape(NZ, RANK, DEPTH), [vmem] * 2, exchange(sketch), all_cores)
    own = call(sample_kernel, shape(NT, RANK, ROWS), [vmem] * 2, exchange(first), left)
    other = lax.ppermute(own, "core", swap)
    wide = DEPTH + 2 * RANK
    stacked = call(gram_kernel, shape(NT, RANK, wide), [vmem] * 3, own, other, left)
    second = call(second_kernel, shape(NZ, RANK, wide), [vmem] * 2, exchange(stacked), all_cores)
    half = (NT, RANK, HALF)
    basis, keep, send = call(
        final_kernel,
        (shape(*half, dtype=F32), shape(*half, dtype=F32), shape(*half)),
        [smem] + [vmem] * 4,
        side,
        exchange(second),
        own,
        other,
        right,
    )
    update = keep + lax.ppermute(send, "core", swap).astype(F32)
    return jnp.transpose(basis, (2, 0, 1)), jnp.transpose(update, (2, 0, 1))


def solution(mesh):
    fine = Mesh(mesh.devices.reshape(8, 2, 4, 8), ("z", "core", "x", "y"))
    layer, col = ("z", "core"), ("x", "y")
    placed = (
        P(layer, col, None, None),
        P(layer, None, None),
        P(col, None),
        P(None, col, None),
    )
    return jax.shard_map(
        local,
        mesh=fine,
        in_specs=placed,
        out_specs=(P(layer, col, None), P(layer, col, None)),
        check_vma=False,
    )
```

```python
import math

import jax
import jax.numpy as jnp
from jax import lax
from jax.experimental import pallas as pl
from jax.experimental.pallas import tpu as pltpu
from jax.sharding import Mesh, PartitionSpec as P

F32 = jnp.float32
BF16 = jnp.bfloat16
HIGHEST = lax.Precision.HIGHEST

NZ = 8
NT = 8
RANK = 64
PANELS = 8
DEPTH = PANELS * RANK
PART = 128
MAIN = DEPTH - PART
ROWS = 256
HALF = 128


def nt_dot(a, b, precision=None):
    return lax.dot_general(
        a, b, (((1,), (1,)), ((), ())), precision=precision, preferred_element_type=F32
    )


def nn_dot(a, b, precision=None):
    return lax.dot_general(
        a, b, (((1,), (0,)), ((), ())), precision=precision, preferred_element_type=F32
    )


def split3(x):
    hi = x.astype(BF16)
    rest = x - hi.astype(F32)
    mid = rest.astype(BF16)
    low = (rest - mid.astype(F32)).astype(BF16)
    return hi, mid, low


def slice_kernel(f_ref, o_ref):
    o_ref[0] = f_ref[...]


def sketch_kernel(first_ref, second_ref, z_ref, f_ref, g_ref, probe_ref, cores_ref, o_ref, left_ref, right_ref,
                  slot_ref, sem_right, sem_left, sem_probe):
    start = pl.multiple_of(z_ref[0] * ROWS, ROWS)
    def fetch(rows_ref, t, out_ref, sem):
        block = rows_ref[t]
        return (
            pltpu.make_async_copy(f_ref.at[block], out_ref.at[t, 0:MAIN], sem.at[t, 0]),
            pltpu.make_async_copy(g_ref.at[block], out_ref.at[t, MAIN:DEPTH], sem.at[t, 1]),
        )

    rights, lefts = [], []
    for t in range(NT):
        probe = pltpu.make_async_copy(probe_ref.at[t, :, pl.ds(start, ROWS)], slot_ref.at[t], sem_probe.at[t])
        rights.append(fetch(second_ref, t, right_ref, sem_right) + (probe,))
        lefts.append(fetch(first_ref, t, left_ref, sem_left))
    for group in rights + lefts:
        for copy in group:
            copy.start()
    for t in range(NT):
        for copy in rights[t]:
            copy.wait()
        o_ref[t] = nt_dot(slot_ref[t], right_ref[t]).astype(BF16)
    for group in lefts:
        for copy in group:
            copy.wait()


def core_products(total, cores_ref):
    parts = []
    for k in range(PANELS):
        block = total[:, k * RANK:(k + 1) * RANK]
        parts.append(nt_dot(block, cores_ref[k], HIGHEST))
    return parts


def first_kernel(part_ref, cores_ref, o_ref):
    total = part_ref[0].astype(F32)
    for q in range(1, NZ):
        total = total + part_ref[q].astype(F32)
    parts = core_products(total, cores_ref)
    for k in range(PANELS):
        half = parts[k].astype(BF16)
        for q in range(NZ):
            o_ref[q, :, k * RANK:(k + 1) * RANK] = half


def sample_kernel(core_ref, f_ref, o_ref):
    for t in range(NT):
        o_ref[t] = nn_dot(core_ref[t], f_ref[t]).astype(BF16)


def pack_gram(gram):
    row = lax.broadcasted_iota(jnp.int32, (RANK, RANK), 0)
    col = lax.broadcasted_iota(jnp.int32, (RANK, RANK), 1)
    one, two, three = (part.astype(F32) for part in split3(gram))
    diag = jnp.sum(jnp.where(row == col, two, 0.0), axis=1, keepdims=True)
    last = jnp.sum(jnp.where((row == RANK - 1) & (col == RANK - 1), two, 0.0), axis=(0, 1), keepdims=True)
    upper = jnp.where(col == row + 1, diag, 0.0)
    upper = jnp.where((row == 0) & (col == RANK - 1), last, upper)
    return jnp.where(col <= row, one, jnp.transpose(two)), jnp.where(col <= row, three, upper)


def unpack_gram(left, right):
    row = lax.broadcasted_iota(jnp.int32, (RANK, RANK), 0)
    col = lax.broadcasted_iota(jnp.int32, (RANK, RANK), 1)
    corner = (row == 0) & (col == RANK - 1)
    last = jnp.sum(jnp.where(corner, right, 0.0), axis=(0, 1), keepdims=True)
    diag = jnp.sum(jnp.where(col == row + 1, right, 0.0), axis=1, keepdims=True)
    two_diag = jnp.where((row == col) & (row < RANK - 1), diag, 0.0)
    two_diag = jnp.where((row == RANK - 1) & (col == RANK - 1), last, two_diag)
    lower = col <= row
    one = jnp.where(lower, left, 0.0)
    three = jnp.where(lower, right, 0.0)
    two = jnp.where(col > row, left, 0.0)
    strict = jnp.where(col < row, one, 0.0) + jnp.where(col < row, three, 0.0)
    full_diag = jnp.where(row == col, one + (three + two_diag), 0.0)
    below = strict + jnp.where(col < row, jnp.transpose(two), 0.0)
    return below + full_diag + jnp.transpose(below)


def gram_kernel(own_ref, other_ref, f_ref, o_ref):
    for t in range(NT):
        total = own_ref[t].astype(F32) + other_ref[t].astype(F32)
        gram = nt_dot(total, total, HIGHEST)
        hi = total.astype(BF16)
        low = (total - hi.astype(F32)).astype(BF16)
        both = nt_dot(jnp.concatenate([hi, low], axis=0), f_ref[t])
        o_ref[t, :, 0:DEPTH] = (both[0:RANK] + both[RANK:2 * RANK]).astype(BF16)
        left, right = pack_gram(gram)
        o_ref[t, :, DEPTH:DEPTH + 2 * RANK] = jnp.concatenate([left, right], axis=1).astype(BF16)


def inverse_factor(gram):
    row_id = lax.broadcasted_iota(jnp.int32, (RANK, RANK), 0)
    col_id = lax.broadcasted_iota(jnp.int32, (RANK, RANK), 1)
    unit = jnp.where(row_id == col_id, 1.0, 0.0).astype(F32)
    work = jnp.concatenate([gram, unit], axis=1)
    blocks = [work[8 * b:8 * b + 8, :] for b in range(RANK // 8)]
    sub = lax.broadcasted_iota(jnp.int32, (8, 2 * RANK), 0)
    scales = []
    for p in range(RANK):
        home, at = divmod(p, 8)
        row = blocks[home][at:at + 1, :]
        pivot = row[:, p:p + 1]
        scaled = row * (1.0 / pivot)
        for b in range(home, RANK // 8):
            col = jnp.broadcast_to(blocks[b][:, p:p + 1], (8, 2 * RANK))
            if b == home:
                col = jnp.where(sub > at, col, 0.0)
            blocks[b] = blocks[b] - col * scaled
    work = jnp.concatenate(blocks, axis=0)
    diag = jnp.sum(jnp.where(row_id == col_id, work[:, 0:RANK], 0.0), axis=1, keepdims=True)
    return work[:, RANK:2 * RANK] * (1.0 / jnp.sqrt(diag))


def second_kernel(part_ref, cores_ref, o_ref):
    total = part_ref[0, :, 0:DEPTH].astype(F32)
    for q in range(1, NZ):
        total = total + part_ref[q, :, 0:DEPTH].astype(F32)
    packed = part_ref[0, :, DEPTH:DEPTH + 2 * RANK].astype(F32)
    for q in range(1, NZ):
        packed = packed + part_ref[q, :, DEPTH:DEPTH + 2 * RANK].astype(F32)
    gram = unpack_gram(packed[:, 0:RANK], packed[:, RANK:2 * RANK])
    inverse = inverse_factor(gram)
    projected = nn_dot(inverse, total, HIGHEST)
    parts = core_products(projected, cores_ref)
    one, two, _ = split3(inverse)
    for q in range(NZ):
        for k in range(PANELS):
            o_ref[q, :, k * RANK:(k + 1) * RANK] = parts[k].astype(BF16)
        o_ref[q, :, DEPTH:DEPTH + RANK] = one
        o_ref[q, :, DEPTH + RANK:DEPTH + 2 * RANK] = two


def final_kernel(side_ref, core_ref, own_ref, other_ref, f_ref, basis_ref, keep_ref, send_ref):
    upper = side_ref[0] == 1
    for t in range(NT):
        inverse = core_ref[t, :, DEPTH:DEPTH + RANK].astype(F32)
        inverse = inverse + core_ref[t, :, DEPTH + RANK:DEPTH + 2 * RANK].astype(F32)
        total = own_ref[t].astype(F32) + other_ref[t].astype(F32)
        half = jnp.where(upper, total[:, HALF:ROWS], total[:, 0:HALF])
        basis_ref[t] = nn_dot(inverse, half, HIGHEST) * math.sqrt(2048.0)
        part = nn_dot(core_ref[t, :, 0:DEPTH], f_ref[t])
        first, last = part[:, 0:HALF], part[:, HALF:ROWS]
        keep_ref[t] = jnp.where(upper, last, first)
        send_ref[t] = jnp.where(upper, first, last).astype(BF16)


def in_hbm(x):
    return pltpu.with_memory_space_constraint(x, pltpu.HBM)


def local(factors, cores, tile_list, probes):
    swap = [(0, 1), (1, 0)]
    z = lax.axis_index("z").astype(jnp.int32).reshape(1)
    side = lax.axis_index("core").astype(jnp.int32).reshape(1)
    row_first = tile_list[:, 0].astype(jnp.int32)
    row_second = tile_list[:, 1].astype(jnp.int32)
    params = pltpu.CompilerParams(vmem_limit_bytes=32 * 1024 * 1024)

    smem = pl.BlockSpec(memory_space=pltpu.SMEM)
    hbm = pl.BlockSpec(memory_space=pl.ANY)
    vmem = pl.BlockSpec(memory_space=pltpu.VMEM)

    def call(kernel, out_shape, in_specs, *args, scratch=()):
        return pl.pallas_call(
            kernel,
            out_shape=out_shape,
            in_specs=in_specs,
            out_specs=jax.tree.map(lambda _: vmem, out_shape),
            scratch_shapes=scratch,
            compiler_params=params,
        )(*args)

    def shape(*dims, dtype=BF16):
        return jax.ShapeDtypeStruct(dims, dtype)

    def exchange(x):
        return lax.all_to_all(x, "z", 0, 0, tiled=True)

    mine = jnp.transpose(factors[0, 0], (1, 0))
    sliced = pl.pallas_call(
        slice_kernel,
        out_shape=shape(NZ, RANK, ROWS),
        grid=(NZ,),
        in_specs=[pl.BlockSpec((RANK, ROWS), lambda t: (0, t))],
        out_specs=pl.BlockSpec((1, RANK, ROWS), lambda t: (t, 0, 0)),
        compiler_params=params,
    )(mine)
    panels = exchange(sliced).reshape(DEPTH, ROWS)
    col = ("x", "y")
    gathered = in_hbm(lax.all_gather(panels[:MAIN], col, axis=0, tiled=False))
    copies = jnp.broadcast_to(panels[MAIN:], (lax.axis_size(col), PART, ROWS))
    beside = in_hbm(lax.all_to_all(copies, col, 0, 0, tiled=True))
    core, _ = lax.optimization_barrier((cores[0], panels))
    all_cores = lax.all_gather(core, "z", axis=0, tiled=False)

    probe = in_hbm(jnp.transpose(probes, (1, 2, 0)))
    block = shape(NT, DEPTH, ROWS)
    sketch, left, right = call(
        sketch_kernel,
        (shape(NT, RANK, DEPTH), block, block),
        [smem, smem, smem, hbm, hbm, hbm, hbm],
        row_first,
        row_second,
        z,
        gathered,
        beside,
        probe,
        all_cores,
        scratch=[pltpu.VMEM((NT, RANK, ROWS), BF16)] + [
            pltpu.SemaphoreType.DMA((NT, 2)),
            pltpu.SemaphoreType.DMA((NT, 2)),
            pltpu.SemaphoreType.DMA((NT,)),
        ],
    )
    first = call(first_kernel, shape(NZ, RANK, DEPTH), [vmem] * 2, exchange(sketch), all_cores)
    own = call(sample_kernel, shape(NT, RANK, ROWS), [vmem] * 2, exchange(first), left)
    other = lax.ppermute(own, "core", swap)
    wide = DEPTH + 2 * RANK
    stacked = call(gram_kernel, shape(NT, RANK, wide), [vmem] * 3, own, other, left)
    second = call(second_kernel, shape(NZ, RANK, wide), [vmem] * 2, exchange(stacked), all_cores)
    half = (NT, RANK, HALF)
    basis, keep, send = call(
        final_kernel,
        (shape(*half, dtype=F32), shape(*half, dtype=F32), shape(*half)),
        [smem] + [vmem] * 4,
        side,
        exchange(second),
        own,
        other,
        right,
    )
    update = keep + lax.ppermute(send, "core", swap).astype(F32)
    return jnp.transpose(basis, (2, 0, 1)), jnp.transpose(update, (2, 0, 1))


def solution(mesh):
    fine = Mesh(mesh.devices.reshape(8, 2, 4, 8), ("z", "core", "x", "y"))
    layer, col = ("z", "core"), ("x", "y")
    placed = (
        P(layer, col, None, None),
        P(layer, None, None),
        P(col, None),
        P(None, col, None),
    )
    return jax.shard_map(
        local,
        mesh=fine,
        in_specs=placed,
        out_specs=(P(layer, col, None), P(layer, col, None)),
        check_vma=False,
    )
```

```python
import math

import jax
import jax.numpy as jnp
from jax import lax
from jax.experimental import pallas as pl
from jax.experimental.pallas import tpu as pltpu
from jax.sharding import Mesh, PartitionSpec as P

F32 = jnp.float32
BF16 = jnp.bfloat16
HIGHEST = lax.Precision.HIGHEST

NZ = 8
NT = 8
RANK = 64
PANELS = 8
DEPTH = PANELS * RANK
ROWS = 256
HALF = 128
BUNDLES = 10


def nt_dot(a, b, precision=None):
    return lax.dot_general(
        a, b, (((1,), (1,)), ((), ())), precision=precision, preferred_element_type=F32
    )


def nn_dot(a, b, precision=None):
    return lax.dot_general(
        a, b, (((1,), (0,)), ((), ())), precision=precision, preferred_element_type=F32
    )


def split3(x):
    hi = x.astype(BF16)
    rest = x - hi.astype(F32)
    mid = rest.astype(BF16)
    low = (rest - mid.astype(F32)).astype(BF16)
    return hi, mid, low


def slice_kernel(f_ref, cores_ref, o_ref):
    one, two, _ = split3(cores_ref[...])
    both = jnp.concatenate([one, two], axis=1)
    for q in range(NZ):
        o_ref[q, :, 0:ROWS] = f_ref[:, q * ROWS:(q + 1) * ROWS]
        o_ref[q, :, ROWS:ROWS + 2 * RANK] = both


def in_hbm(x):
    return pltpu.with_memory_space_constraint(x, pltpu.HBM)


def spread(own):
    def send(value, x_step, y_step):
        pairs = []
        for x in range(4):
            for y in range(8):
                if x_step is not None:
                    pairs.append((x * 8 + y, (x + x_step) % 4 * 8 + y))
                if y_step is not None:
                    pairs.append((32 + x * 8 + y, 32 + x * 8 + (y + y_step) % 8))
        return lax.ppermute(value, ("core", "x", "y"), pairs)

    def bundle_send(value, y_step, x_step):
        pairs = []
        for x in range(4):
            for y in range(8):
                pairs.append((x * 8 + y, x * 8 + (y + y_step) % 8))
                if x_step is not None:
                    pairs.append((32 + x * 8 + y, 32 + (x + x_step) % 4 * 8 + y))
        return lax.ppermute(value, ("core", "x", "y"), pairs)

    lower = lax.axis_index("core") == 0
    steps = [(1, 1), (-1, -1), (2, 2), (None, -2), (None, 3), (None, -3), (None, 4)]
    single = [send(own, *step) for step in steps]
    near = jnp.stack([own] + single[0:3])
    far = jnp.stack(single[3:7])
    out1 = bundle_send(near, 1, 1)
    out2 = bundle_send(near, -1, -1)
    out3 = bundle_send(jnp.where(lower, out1, far), 1, 1)
    out4 = bundle_send(jnp.where(lower, out2, far), -1, -1)
    out5 = bundle_send(jnp.where(lower, out3, out1), 1, 1)
    out6 = bundle_send(out4, -1, -1)
    out7 = bundle_send(out5[0:2], 1, None)
    out8 = bundle_send(out6[2:4], -1, None)
    return near, far, out1, out2, out3, out4, out5, out6, out7, out8


def pick(index, *values):
    out = jnp.full_like(index, values[0])
    for number, value in enumerate(values[1:], 1):
        out = jnp.where(index == number, value, out)
    return out


def locate(rows):
    dx = (lax.axis_index("x").astype(jnp.int32) - rows // 8) % 4
    dy = (lax.axis_index("y").astype(jnp.int32) - rows % 8) % 8
    place = pick(dx, 0, 1, 3, 2)
    by_y = pick(dy, 0, 2, 4, 6, 8, 7, 5, 3)
    across = (dy == 4) & (place >= 2)
    which0 = jnp.where(across, 9, by_y)
    place0 = jnp.where(across, place - 2, place)
    place1 = pick(dy, 0, 1, 3, 1, 3, 2, 0, 2)
    which1 = jnp.where((dy <= 2) | (dy == 7), pick(dx, 0, 2, 6, 3), pick(dx, 1, 4, 7, 5))
    lower = lax.axis_index("core") == 0
    return jnp.where(lower, which0, which1), jnp.where(lower, place0, place1)


def sketch_kernel(first_ref, second_ref, z_ref, probe_ref, *refs):
    bundles, refs = refs[0:BUNDLES], refs[BUNDLES:]
    o_ref, left_ref, right_ref, slot_ref, sem_right, sem_left, sem_probe = refs
    start = pl.multiple_of(z_ref[0] * ROWS, ROWS)

    def fetch(place_ref, t, out_ref, sem):
        which, at = place_ref[0, t], place_ref[1, t]
        for number, bundle in enumerate(bundles):

            @pl.when(which == number)
            def _():
                pltpu.make_async_copy(bundle.at[at], out_ref.at[t], sem.at[t]).start()

    def arrived(t, out_ref, sem):
        pltpu.make_async_copy(bundles[0].at[0], out_ref.at[t], sem.at[t]).wait()

    probes = []
    for t in range(NT):
        probes.append(
            pltpu.make_async_copy(probe_ref.at[t, :, pl.ds(start, ROWS)], slot_ref.at[t], sem_probe.at[t])
        )
        probes[t].start()
        fetch(second_ref, t, right_ref, sem_right)
    for t in range(NT):
        fetch(first_ref, t, left_ref, sem_left)
    for t in range(NT):
        probes[t].wait()
        arrived(t, right_ref, sem_right)
        o_ref[t] = nt_dot(slot_ref[t], right_ref[t]).astype(BF16)
    for t in range(NT):
        arrived(t, left_ref, sem_left)


def core_products(total, cores_ref):
    parts = []
    for k in range(PANELS):
        block = total[:, k * RANK:(k + 1) * RANK]
        parts.append(nt_dot(block, cores_ref[k], HIGHEST))
    return parts


def first_kernel(part_ref, cores_ref, o_ref):
    total = part_ref[0].astype(F32)
    for q in range(1, NZ):
        total = total + part_ref[q].astype(F32)
    parts = core_products(total, cores_ref)
    for k in range(PANELS):
        half = parts[k].astype(BF16)
        for q in range(NZ):
            o_ref[q, :, k * RANK:(k + 1) * RANK] = half


def sample_kernel(core_ref, f_ref, o_ref):
    for t in range(NT):
        o_ref[t] = nn_dot(core_ref[t], f_ref[t]).astype(BF16)


def pack_gram(gram):
    row = lax.broadcasted_iota(jnp.int32, (RANK, RANK), 0)
    col = lax.broadcasted_iota(jnp.int32, (RANK, RANK), 1)
    one, two, three = (part.astype(F32) for part in split3(gram))
    diag = jnp.sum(jnp.where(row == col, two, 0.0), axis=1, keepdims=True)
    last = jnp.sum(jnp.where((row == RANK - 1) & (col == RANK - 1), two, 0.0), axis=(0, 1), keepdims=True)
    upper = jnp.where(col == row + 1, diag, 0.0)
    upper = jnp.where((row == 0) & (col == RANK - 1), last, upper)
    return jnp.where(col <= row, one, jnp.transpose(two)), jnp.where(col <= row, three, upper)


def unpack_gram(left, right):
    row = lax.broadcasted_iota(jnp.int32, (RANK, RANK), 0)
    col = lax.broadcasted_iota(jnp.int32, (RANK, RANK), 1)
    corner = (row == 0) & (col == RANK - 1)
    last = jnp.sum(jnp.where(corner, right, 0.0), axis=(0, 1), keepdims=True)
    diag = jnp.sum(jnp.where(col == row + 1, right, 0.0), axis=1, keepdims=True)
    two_diag = jnp.where((row == col) & (row < RANK - 1), diag, 0.0)
    two_diag = jnp.where((row == RANK - 1) & (col == RANK - 1), last, two_diag)
    lower = col <= row
    one = jnp.where(lower, left, 0.0)
    three = jnp.where(lower, right, 0.0)
    two = jnp.where(col > row, left, 0.0)
    strict = jnp.where(col < row, one, 0.0) + jnp.where(col < row, three, 0.0)
    full_diag = jnp.where(row == col, one + (three + two_diag), 0.0)
    below = strict + jnp.where(col < row, jnp.transpose(two), 0.0)
    return below + full_diag + jnp.transpose(below)


def gram_kernel(own_ref, other_ref, f_ref, o_ref):
    for t in range(NT):
        total = own_ref[t].astype(F32) + other_ref[t].astype(F32)
        gram = nt_dot(total, total, HIGHEST)
        hi = total.astype(BF16)
        low = (total - hi.astype(F32)).astype(BF16)
        both = nt_dot(jnp.concatenate([hi, low], axis=0), f_ref[t])
        o_ref[t, :, 0:DEPTH] = (both[0:RANK] + both[RANK:2 * RANK]).astype(BF16)
        left, right = pack_gram(gram)
        o_ref[t, :, DEPTH:DEPTH + 2 * RANK] = jnp.concatenate([left, right], axis=1).astype(BF16)


def inverse_factor(gram):
    row_id = lax.broadcasted_iota(jnp.int32, (RANK, RANK), 0)
    col_id = lax.broadcasted_iota(jnp.int32, (RANK, RANK), 1)
    unit = jnp.where(row_id == col_id, 1.0, 0.0).astype(F32)
    work = jnp.concatenate([gram, unit], axis=1)
    blocks = [work[8 * b:8 * b + 8, :] for b in range(RANK // 8)]
    sub = lax.broadcasted_iota(jnp.int32, (8, 2 * RANK), 0)
    scales = []
    for p in range(RANK):
        home, at = divmod(p, 8)
        row = blocks[home][at:at + 1, :]
        pivot = row[:, p:p + 1]
        scaled = row * (1.0 / pivot)
        for b in range(home, RANK // 8):
            col = jnp.broadcast_to(blocks[b][:, p:p + 1], (8, 2 * RANK))
            if b == home:
                col = jnp.where(sub > at, col, 0.0)
            blocks[b] = blocks[b] - col * scaled
    work = jnp.concatenate(blocks, axis=0)
    diag = jnp.sum(jnp.where(row_id == col_id, work[:, 0:RANK], 0.0), axis=1, keepdims=True)
    return work[:, RANK:2 * RANK] * (1.0 / jnp.sqrt(diag))


def second_kernel(part_ref, cores_ref, o_ref):
    total = part_ref[0, :, 0:DEPTH].astype(F32)
    for q in range(1, NZ):
        total = total + part_ref[q, :, 0:DEPTH].astype(F32)
    packed = part_ref[0, :, DEPTH:DEPTH + 2 * RANK].astype(F32)
    for q in range(1, NZ):
        packed = packed + part_ref[q, :, DEPTH:DEPTH + 2 * RANK].astype(F32)
    gram = unpack_gram(packed[:, 0:RANK], packed[:, RANK:2 * RANK])
    inverse = inverse_factor(gram)
    projected = nn_dot(inverse, total, HIGHEST)
    parts = core_products(projected, cores_ref)
    one, two, _ = split3(inverse)
    for q in range(NZ):
        for k in range(PANELS):
            o_ref[q, :, k * RANK:(k + 1) * RANK] = parts[k].astype(BF16)
        o_ref[q, :, DEPTH:DEPTH + RANK] = one
        o_ref[q, :, DEPTH + RANK:DEPTH + 2 * RANK] = two


def final_kernel(side_ref, core_ref, own_ref, other_ref, f_ref, basis_ref, keep_ref, send_ref):
    upper = side_ref[0] == 1
    for t in range(NT):
        inverse = core_ref[t, :, DEPTH:DEPTH + RANK].astype(F32)
        inverse = inverse + core_ref[t, :, DEPTH + RANK:DEPTH + 2 * RANK].astype(F32)
        total = own_ref[t].astype(F32) + other_ref[t].astype(F32)
        half = jnp.where(upper, total[:, HALF:ROWS], total[:, 0:HALF])
        basis_ref[t] = nn_dot(inverse, half, HIGHEST) * math.sqrt(2048.0)
        part = nn_dot(core_ref[t, :, 0:DEPTH], f_ref[t])
        first, last = part[:, 0:HALF], part[:, HALF:ROWS]
        keep_ref[t] = jnp.where(upper, last, first)
        send_ref[t] = jnp.where(upper, first, last).astype(BF16)


def local(factors, cores, tile_list, probes):
    swap = [(0, 1), (1, 0)]
    z = lax.axis_index("z").astype(jnp.int32).reshape(1)
    side = lax.axis_index("core").astype(jnp.int32).reshape(1)
    row_first = tile_list[:, 0].astype(jnp.int32)
    row_second = tile_list[:, 1].astype(jnp.int32)
    params = pltpu.CompilerParams(vmem_limit_bytes=32 * 1024 * 1024)

    smem = pl.BlockSpec(memory_space=pltpu.SMEM)
    hbm = pl.BlockSpec(memory_space=pl.ANY)
    vmem = pl.BlockSpec(memory_space=pltpu.VMEM)

    def call(kernel, out_shape, in_specs, *args, scratch=()):
        return pl.pallas_call(
            kernel,
            out_shape=out_shape,
            in_specs=in_specs,
            out_specs=jax.tree.map(lambda _: vmem, out_shape),
            scratch_shapes=scratch,
            compiler_params=params,
        )(*args)

    def shape(*dims, dtype=BF16):
        return jax.ShapeDtypeStruct(dims, dtype)

    def exchange(x):
        return lax.all_to_all(x, "z", 0, 0, tiled=True)

    mine = jnp.transpose(factors[0, 0], (1, 0))
    sliced = call(slice_kernel, shape(NZ, RANK, ROWS + 2 * RANK), [vmem] * 2, mine, cores[0])
    panels = exchange(sliced)
    pieces = panels[:, :, ROWS:ROWS + 2 * RANK].astype(F32)
    all_cores = pieces[:, :, 0:RANK] + pieces[:, :, RANK:2 * RANK]
    bundles = spread(panels[:, :, 0:ROWS].reshape(DEPTH, ROWS))
    probe = in_hbm(jnp.transpose(probes, (1, 2, 0)))
    block = shape(NT, DEPTH, ROWS)
    sketch, left, right = call(
        sketch_kernel,
        (shape(NT, RANK, DEPTH), block, block),
        [smem, smem, smem] + [hbm] * (1 + BUNDLES),
        jnp.stack(locate(row_first)),
        jnp.stack(locate(row_second)),
        z,
        probe,
        *(in_hbm(bundle) for bundle in bundles),
        scratch=[pltpu.VMEM((NT, RANK, ROWS), BF16)] + [pltpu.SemaphoreType.DMA((NT,))] * 3,
    )
    first = call(first_kernel, shape(NZ, RANK, DEPTH), [vmem] * 2, exchange(sketch), all_cores)
    own = call(sample_kernel, shape(NT, RANK, ROWS), [vmem] * 2, exchange(first), left)
    other = lax.ppermute(own, "core", swap)
    wide = DEPTH + 2 * RANK
    stacked = call(gram_kernel, shape(NT, RANK, wide), [vmem] * 3, own, other, left)
    second = call(second_kernel, shape(NZ, RANK, wide), [vmem] * 2, exchange(stacked), all_cores)
    half = (NT, RANK, HALF)
    basis, keep, send = call(
        final_kernel,
        (shape(*half, dtype=F32), shape(*half, dtype=F32), shape(*half)),
        [smem] + [vmem] * 4,
        side,
        exchange(second),
        own,
        other,
        right,
    )
    update = keep + lax.ppermute(send, "core", swap).astype(F32)
    return jnp.transpose(basis, (2, 0, 1)), jnp.transpose(update, (2, 0, 1))


def solution(mesh):
    fine = Mesh(mesh.devices.reshape(8, 2, 4, 8), ("z", "core", "x", "y"))
    layer, col = ("z", "core"), ("x", "y")
    placed = (
        P(layer, col, None, None),
        P(layer, None, None),
        P(col, None),
        P(None, col, None),
    )
    return jax.shard_map(
        local,
        mesh=fine,
        in_specs=placed,
        out_specs=(P(layer, col, None), P(layer, col, None)),
        check_vma=False,
    )
```

```python
import math

import jax
import jax.numpy as jnp
from jax import lax
from jax.experimental import pallas as pl
from jax.experimental.pallas import tpu as pltpu
from jax.sharding import Mesh, PartitionSpec as P

F32 = jnp.float32
BF16 = jnp.bfloat16
HIGHEST = lax.Precision.HIGHEST

NZ = 8
NT = 8
RANK = 64
PANELS = 8
DEPTH = PANELS * RANK
ROWS = 256
HALF = 128
BUNDLES = 10


def nt_dot(a, b, precision=None):
    return lax.dot_general(
        a, b, (((1,), (1,)), ((), ())), precision=precision, preferred_element_type=F32
    )


def nn_dot(a, b, precision=None):
    return lax.dot_general(
        a, b, (((1,), (0,)), ((), ())), precision=precision, preferred_element_type=F32
    )


def split3(x):
    hi = x.astype(BF16)
    rest = x - hi.astype(F32)
    mid = rest.astype(BF16)
    low = (rest - mid.astype(F32)).astype(BF16)
    return hi, mid, low


def slice_kernel(f_ref, cores_ref, o_ref, sem):
    copies = []
    for q in range(NZ):
        copies.append(
            pltpu.make_async_copy(
                f_ref.at[:, q * ROWS:(q + 1) * ROWS], o_ref.at[q, :, 0:ROWS], sem.at[q]
            )
        )
        copies[q].start()
    one, two, _ = split3(cores_ref[...])
    both = jnp.concatenate([one, two], axis=1)
    for q in range(NZ):
        o_ref[q, :, ROWS:ROWS + 2 * RANK] = both
    for copy in copies:
        copy.wait()


def in_hbm(x):
    return pltpu.with_memory_space_constraint(x, pltpu.HBM)


def spread(own):
    def send(value, x_step, y_step):
        pairs = []
        for x in range(4):
            for y in range(8):
                if x_step is not None:
                    pairs.append((x * 8 + y, (x + x_step) % 4 * 8 + y))
                pairs.append((32 + x * 8 + y, 32 + x * 8 + (y + y_step) % 8))
        return lax.ppermute(value, ("core", "x", "y"), pairs)

    def bundle_send(value, y_step, x_step):
        pairs = []
        for x in range(4):
            for y in range(8):
                pairs.append((x * 8 + y, x * 8 + (y + y_step) % 8))
                if x_step is not None:
                    pairs.append((32 + x * 8 + y, 32 + (x + x_step) % 4 * 8 + y))
        return lax.ppermute(value, ("core", "x", "y"), pairs)

    lower = lax.axis_index("core") == 0
    up1 = send(own, 1, 1)
    down1 = send(own, -1, -1)
    up2 = send(up1, 1, 1)
    down2 = send(down1, None, -1)
    up3 = send(up2, None, 1)
    down3 = send(down2, None, -1)
    up4 = send(up3, None, 1)
    single = [up1, down1, up2, down2, up3, down3, up4]
    near = jnp.stack([own] + single[0:3])
    far = jnp.stack(single[3:7])
    out1 = bundle_send(near, 1, 1)
    out2 = bundle_send(near, -1, -1)
    out3 = bundle_send(jnp.where(lower, out1, far), 1, 1)
    out4 = bundle_send(jnp.where(lower, out2, far), -1, -1)
    out5 = bundle_send(jnp.where(lower, out3, out1), 1, 1)
    out6 = bundle_send(out4, -1, -1)
    out7 = bundle_send(out5[0:2], 1, None)
    out8 = bundle_send(out6[2:4], -1, None)
    return near, far, out1, out2, out3, out4, out5, out6, out7, out8


def pick(index, *values):
    out = jnp.full_like(index, values[0])
    for number, value in enumerate(values[1:], 1):
        out = jnp.where(index == number, value, out)
    return out


def locate(rows):
    dx = (lax.axis_index("x").astype(jnp.int32) - rows // 8) % 4
    dy = (lax.axis_index("y").astype(jnp.int32) - rows % 8) % 8
    place = pick(dx, 0, 1, 3, 2)
    by_y = pick(dy, 0, 2, 4, 6, 8, 7, 5, 3)
    across = (dy == 4) & (place >= 2)
    which0 = jnp.where(across, 9, by_y)
    place0 = jnp.where(across, place - 2, place)
    place1 = pick(dy, 0, 1, 3, 1, 3, 2, 0, 2)
    which1 = jnp.where((dy <= 2) | (dy == 7), pick(dx, 0, 2, 6, 3), pick(dx, 1, 4, 7, 5))
    lower = lax.axis_index("core") == 0
    return jnp.where(lower, which0, which1), jnp.where(lower, place0, place1)


def sketch_kernel(first_ref, second_ref, z_ref, probe_ref, *refs):
    bundles, refs = refs[0:BUNDLES], refs[BUNDLES:]
    o_ref, left_ref, right_ref, slot_ref, sem_right, sem_left, sem_probe = refs
    start = pl.multiple_of(z_ref[0] * ROWS, ROWS)

    def fetch(place_ref, t, out_ref, sem):
        which, at = place_ref[0, t], place_ref[1, t]
        for number, bundle in enumerate(bundles):

            @pl.when(which == number)
            def _():
                pltpu.make_async_copy(bundle.at[at], out_ref.at[t], sem.at[t]).start()

    def arrived(t, out_ref, sem):
        pltpu.make_async_copy(bundles[0].at[0], out_ref.at[t], sem.at[t]).wait()

    probes = []
    for t in range(NT):
        probes.append(
            pltpu.make_async_copy(probe_ref.at[t, :, pl.ds(start, ROWS)], slot_ref.at[t], sem_probe.at[t])
        )
        probes[t].start()
        fetch(second_ref, t, right_ref, sem_right)
    for t in range(NT):
        fetch(first_ref, t, left_ref, sem_left)
    for t in range(NT):
        probes[t].wait()
        arrived(t, right_ref, sem_right)
        o_ref[t] = nt_dot(slot_ref[t], right_ref[t]).astype(BF16)
    for t in range(NT):
        arrived(t, left_ref, sem_left)


def core_products(total, cores_ref):
    parts = []
    for k in range(PANELS):
        block = total[:, k * RANK:(k + 1) * RANK]
        parts.append(nt_dot(block, cores_ref[k], HIGHEST))
    return parts


def first_kernel(part_ref, cores_ref, o_ref):
    total = part_ref[0].astype(F32)
    for q in range(1, NZ):
        total = total + part_ref[q].astype(F32)
    parts = core_products(total, cores_ref)
    for k in range(PANELS):
        half = parts[k].astype(BF16)
        for q in range(NZ):
            o_ref[q, :, k * RANK:(k + 1) * RANK] = half


def sample_kernel(core_ref, f_ref, o_ref):
    for t in range(NT):
        o_ref[t] = nn_dot(core_ref[t], f_ref[t]).astype(BF16)


def pack_gram(gram):
    row = lax.broadcasted_iota(jnp.int32, (RANK, RANK), 0)
    col = lax.broadcasted_iota(jnp.int32, (RANK, RANK), 1)
    one, two, three = (part.astype(F32) for part in split3(gram))
    diag = jnp.sum(jnp.where(row == col, two, 0.0), axis=1, keepdims=True)
    last = jnp.sum(jnp.where((row == RANK - 1) & (col == RANK - 1), two, 0.0), axis=(0, 1), keepdims=True)
    upper = jnp.where(col == row + 1, diag, 0.0)
    upper = jnp.where((row == 0) & (col == RANK - 1), last, upper)
    return jnp.where(col <= row, one, jnp.transpose(two)), jnp.where(col <= row, three, upper)


def unpack_gram(left, right):
    row = lax.broadcasted_iota(jnp.int32, (RANK, RANK), 0)
    col = lax.broadcasted_iota(jnp.int32, (RANK, RANK), 1)
    corner = (row == 0) & (col == RANK - 1)
    last = jnp.sum(jnp.where(corner, right, 0.0), axis=(0, 1), keepdims=True)
    diag = jnp.sum(jnp.where(col == row + 1, right, 0.0), axis=1, keepdims=True)
    two_diag = jnp.where((row == col) & (row < RANK - 1), diag, 0.0)
    two_diag = jnp.where((row == RANK - 1) & (col == RANK - 1), last, two_diag)
    lower = col <= row
    one = jnp.where(lower, left, 0.0)
    three = jnp.where(lower, right, 0.0)
    two = jnp.where(col > row, left, 0.0)
    strict = jnp.where(col < row, one, 0.0) + jnp.where(col < row, three, 0.0)
    full_diag = jnp.where(row == col, one + (three + two_diag), 0.0)
    below = strict + jnp.where(col < row, jnp.transpose(two), 0.0)
    return below + full_diag + jnp.transpose(below)


def gram_kernel(own_ref, other_ref, f_ref, o_ref):
    for t in range(NT):
        total = own_ref[t].astype(F32) + other_ref[t].astype(F32)
        gram = nt_dot(total, total, HIGHEST)
        hi = total.astype(BF16)
        low = (total - hi.astype(F32)).astype(BF16)
        both = nt_dot(jnp.concatenate([hi, low], axis=0), f_ref[t])
        o_ref[t, :, 0:DEPTH] = (both[0:RANK] + both[RANK:2 * RANK]).astype(BF16)
        left, right = pack_gram(gram)
        o_ref[t, :, DEPTH:DEPTH + 2 * RANK] = jnp.concatenate([left, right], axis=1).astype(BF16)


def inverse_factor(gram):
    row_id = lax.broadcasted_iota(jnp.int32, (RANK, RANK), 0)
    col_id = lax.broadcasted_iota(jnp.int32, (RANK, RANK), 1)
    unit = jnp.where(row_id == col_id, 1.0, 0.0).astype(F32)
    work = jnp.concatenate([gram, unit], axis=1)
    blocks = [work[8 * b:8 * b + 8, :] for b in range(RANK // 8)]
    sub = lax.broadcasted_iota(jnp.int32, (8, 2 * RANK), 0)
    scales = []
    for p in range(RANK):
        home, at = divmod(p, 8)
        row = blocks[home][at:at + 1, :]
        pivot = row[:, p:p + 1]
        scaled = row * (1.0 / pivot)
        for b in range(home, RANK // 8):
            col = jnp.broadcast_to(blocks[b][:, p:p + 1], (8, 2 * RANK))
            if b == home:
                col = jnp.where(sub > at, col, 0.0)
            blocks[b] = blocks[b] - col * scaled
    work = jnp.concatenate(blocks, axis=0)
    diag = jnp.sum(jnp.where(row_id == col_id, work[:, 0:RANK], 0.0), axis=1, keepdims=True)
    return work[:, RANK:2 * RANK] * (1.0 / jnp.sqrt(diag))


def second_kernel(part_ref, cores_ref, o_ref):
    total = part_ref[0, :, 0:DEPTH].astype(F32)
    for q in range(1, NZ):
        total = total + part_ref[q, :, 0:DEPTH].astype(F32)
    packed = part_ref[0, :, DEPTH:DEPTH + 2 * RANK].astype(F32)
    for q in range(1, NZ):
        packed = packed + part_ref[q, :, DEPTH:DEPTH + 2 * RANK].astype(F32)
    gram = unpack_gram(packed[:, 0:RANK], packed[:, RANK:2 * RANK])
    inverse = inverse_factor(gram)
    projected = nn_dot(inverse, total, HIGHEST)
    parts = core_products(projected, cores_ref)
    one, two, _ = split3(inverse)
    for q in range(NZ):
        for k in range(PANELS):
            o_ref[q, :, k * RANK:(k + 1) * RANK] = parts[k].astype(BF16)
        o_ref[q, :, DEPTH:DEPTH + RANK] = one
        o_ref[q, :, DEPTH + RANK:DEPTH + 2 * RANK] = two


def final_kernel(side_ref, core_ref, own_ref, other_ref, f_ref, basis_ref, keep_ref, send_ref):
    upper = side_ref[0] == 1
    for t in range(NT):
        inverse = core_ref[t, :, DEPTH:DEPTH + RANK].astype(F32)
        inverse = inverse + core_ref[t, :, DEPTH + RANK:DEPTH + 2 * RANK].astype(F32)
        total = own_ref[t].astype(F32) + other_ref[t].astype(F32)
        half = jnp.where(upper, total[:, HALF:ROWS], total[:, 0:HALF])
        basis_ref[t] = nn_dot(inverse, half, HIGHEST) * math.sqrt(2048.0)
        part = nn_dot(core_ref[t, :, 0:DEPTH], f_ref[t])
        first, last = part[:, 0:HALF], part[:, HALF:ROWS]
        keep_ref[t] = jnp.where(upper, last, first)
        send_ref[t] = jnp.where(upper, first, last).astype(BF16)


def local(factors, cores, tile_list, probes):
    swap = [(0, 1), (1, 0)]
    z = lax.axis_index("z").astype(jnp.int32).reshape(1)
    side = lax.axis_index("core").astype(jnp.int32).reshape(1)
    row_first = tile_list[:, 0].astype(jnp.int32)
    row_second = tile_list[:, 1].astype(jnp.int32)
    params = pltpu.CompilerParams(vmem_limit_bytes=32 * 1024 * 1024)

    smem = pl.BlockSpec(memory_space=pltpu.SMEM)
    hbm = pl.BlockSpec(memory_space=pl.ANY)
    vmem = pl.BlockSpec(memory_space=pltpu.VMEM)

    def call(kernel, out_shape, in_specs, *args, scratch=()):
        return pl.pallas_call(
            kernel,
            out_shape=out_shape,
            in_specs=in_specs,
            out_specs=jax.tree.map(lambda _: vmem, out_shape),
            scratch_shapes=scratch,
            compiler_params=params,
        )(*args)

    def shape(*dims, dtype=BF16):
        return jax.ShapeDtypeStruct(dims, dtype)

    def exchange(x):
        return lax.all_to_all(x, "z", 0, 0, tiled=True)

    mine = jnp.transpose(factors[0, 0], (1, 0))
    sliced = call(
        slice_kernel,
        shape(NZ, RANK, ROWS + 2 * RANK),
        [hbm, vmem],
        in_hbm(mine),
        cores[0],
        scratch=[pltpu.SemaphoreType.DMA((NZ,))],
    )
    panels = exchange(sliced)
    pieces = panels[:, :, ROWS:ROWS + 2 * RANK].astype(F32)
    all_cores = pieces[:, :, 0:RANK] + pieces[:, :, RANK:2 * RANK]
    bundles = spread(panels[:, :, 0:ROWS].reshape(DEPTH, ROWS))
    probe = in_hbm(jnp.transpose(probes, (1, 2, 0)))
    block = shape(NT, DEPTH, ROWS)
    sketch, left, right = call(
        sketch_kernel,
        (shape(NT, RANK, DEPTH), block, block),
        [smem, smem, smem] + [hbm] * (1 + BUNDLES),
        jnp.stack(locate(row_first)),
        jnp.stack(locate(row_second)),
        z,
        probe,
        *(in_hbm(bundle) for bundle in bundles),
        scratch=[pltpu.VMEM((NT, RANK, ROWS), BF16)] + [pltpu.SemaphoreType.DMA((NT,))] * 3,
    )
    first = call(first_kernel, shape(NZ, RANK, DEPTH), [vmem] * 2, exchange(sketch), all_cores)
    own = call(sample_kernel, shape(NT, RANK, ROWS), [vmem] * 2, exchange(first), left)
    other = lax.ppermute(own, "core", swap)
    wide = DEPTH + 2 * RANK
    stacked = call(gram_kernel, shape(NT, RANK, wide), [vmem] * 3, own, other, left)
    second = call(second_kernel, shape(NZ, RANK, wide), [vmem] * 2, exchange(stacked), all_cores)
    half = (NT, RANK, HALF)
    basis, keep, send = call(
        final_kernel,
        (shape(*half, dtype=F32), shape(*half, dtype=F32), shape(*half)),
        [smem] + [vmem] * 4,
        side,
        exchange(second),
        own,
        other,
        right,
    )
    update = keep + lax.ppermute(send, "core", swap).astype(F32)
    return jnp.transpose(basis, (2, 0, 1)), jnp.transpose(update, (2, 0, 1))


def solution(mesh):
    fine = Mesh(mesh.devices.reshape(8, 2, 4, 8), ("z", "core", "x", "y"))
    layer, col = ("z", "core"), ("x", "y")
    placed = (
        P(layer, col, None, None),
        P(layer, None, None),
        P(col, None),
        P(None, col, None),
    )
    return jax.shard_map(
        local,
        mesh=fine,
        in_specs=placed,
        out_specs=(P(layer, col, None), P(layer, col, None)),
        check_vma=False,
    )
```

```python
import math

import jax
import jax.numpy as jnp
from jax import lax
from jax.experimental import pallas as pl
from jax.experimental.pallas import tpu as pltpu
from jax.sharding import Mesh, PartitionSpec as P

F32 = jnp.float32
BF16 = jnp.bfloat16
HIGHEST = lax.Precision.HIGHEST

NZ = 8
NT = 8
RANK = 64
PANELS = 8
DEPTH = PANELS * RANK
ROWS = 256
HALF = 128
BUNDLES = 18
EXTRA = 16


def nt_dot(a, b, precision=None):
    return lax.dot_general(
        a, b, (((1,), (1,)), ((), ())), precision=precision, preferred_element_type=F32
    )


def nn_dot(a, b, precision=None):
    return lax.dot_general(
        a, b, (((1,), (0,)), ((), ())), precision=precision, preferred_element_type=F32
    )


def split3(x):
    hi = x.astype(BF16)
    rest = x - hi.astype(F32)
    mid = rest.astype(BF16)
    low = (rest - mid.astype(F32)).astype(BF16)
    return hi, mid, low


def slice_kernel(f_ref, cores_ref, o_ref, sem):
    copies = []
    for q in range(NZ):
        copies.append(
            pltpu.make_async_copy(
                f_ref.at[:, q * ROWS:(q + 1) * ROWS], o_ref.at[q, :, 0:ROWS], sem.at[q]
            )
        )
        copies[q].start()
    one, two, _ = split3(cores_ref[...])
    both = jnp.concatenate([one, two], axis=1)
    for q in range(NZ):
        o_ref[q, :, ROWS:ROWS + 2 * RANK] = both
    for copy in copies:
        copy.wait()


def in_hbm(x):
    return pltpu.with_memory_space_constraint(x, pltpu.HBM)


def spread(own):
    def send(value, x_step, y_step):
        pairs = []
        for x in range(4):
            for y in range(8):
                if x_step is not None:
                    pairs.append((x * 8 + y, (x + x_step) % 4 * 8 + y))
                pairs.append((32 + x * 8 + y, 32 + x * 8 + (y + y_step) % 8))
        return lax.ppermute(value, ("core", "x", "y"), pairs)

    def bundle_send(value, y_step, x_step):
        pairs = []
        for x in range(4):
            for y in range(8):
                pairs.append((x * 8 + y, x * 8 + (y + y_step) % 8))
                if x_step is not None:
                    pairs.append((32 + x * 8 + y, 32 + (x + x_step) % 4 * 8 + y))
        return lax.ppermute(value, ("core", "x", "y"), pairs)

    lower = lax.axis_index("core") == 0
    up1 = send(own, 1, 1)
    down1 = send(own, -1, -1)
    up2 = send(up1, 1, 1)
    down2 = send(down1, None, -1)
    up3 = send(up2, None, 1)
    down3 = send(down2, None, -1)
    up4 = send(up3, None, 1)
    near = [jnp.stack([own, up1]), jnp.stack([down1, up2])]
    far = [jnp.stack([down2, up3]), jnp.stack([down3, up4])]
    out1, out2, out3, out4, out5, out6 = ([None, None] for _ in range(6))
    for h in range(2):
        out1[h] = bundle_send(near[h], 1, 1)
        out2[h] = bundle_send(near[h], -1, -1)
    for h in range(2):
        out3[h] = bundle_send(out1[h], 1, 1)
        out4[h] = bundle_send(jnp.where(lower, out2[h], far[h]), -1, -1)
    for h in range(2):
        out5[h] = bundle_send(jnp.where(lower, out3[h], far[h]), 1, 1)
        out6[1 - h] = bundle_send(out4[1 - h], -1, -1)
    out7 = bundle_send(out5[0], 1, None)
    out8 = bundle_send(out6[1], -1, None)
    return (*near, *far, *out1, *out2, *out3, *out4, *out5, *out6, out7, out8)


def pick(index, *values):
    out = jnp.full_like(index, values[0])
    for number, value in enumerate(values[1:], 1):
        out = jnp.where(index == number, value, out)
    return out


def locate(rows):
    dx = (lax.axis_index("x").astype(jnp.int32) - rows // 8) % 4
    dy = (lax.axis_index("y").astype(jnp.int32) - rows % 8) % 8
    lower = lax.axis_index("core") == 0
    place0 = pick(dx, 0, 1, 3, 2)
    half0 = place0 // 2
    which0 = pick(dy, 0, 4, 8, 12, 16, 14, 10, 6) + half0
    place1 = pick(dy, 0, 1, 3, 1, 3, 2, 0, 2)
    half1 = place1 // 2
    which1 = jnp.where((dy <= 2) | (dy == 7), pick(dx, 0, 4, 8, 6), pick(dx, 2, 12, 14, 10)) + half1
    return jnp.where(lower, which0, which1), jnp.where(lower, place0 - 2 * half0, place1 - 2 * half1)


def sketch_kernel(first_ref, second_ref, z_ref, probe_ref, *refs):
    bundles, refs = refs[0:BUNDLES], refs[BUNDLES:]
    o_ref, left_ref, right_ref, slot_ref, sem_right, sem_left, sem_probe = refs
    start = pl.multiple_of(z_ref[0] * ROWS, ROWS)

    def fetch(place_ref, t, out_ref, sem):
        which, at = place_ref[0, t], place_ref[1, t]

        def choose(low, high):
            if high - low == 1:
                pltpu.make_async_copy(bundles[low].at[at], out_ref.at[t], sem.at[t]).start()
                return
            middle = (low + high) // 2

            @pl.when(which < middle)
            def _():
                choose(low, middle)

            @pl.when(which >= middle)
            def _():
                choose(middle, high)

        choose(0, BUNDLES)

    def arrived(t, out_ref, sem):
        pltpu.make_async_copy(bundles[0].at[0], out_ref.at[t], sem.at[t]).wait()

    probes = []
    for t in range(NT):
        probes.append(
            pltpu.make_async_copy(probe_ref.at[t, :, pl.ds(start, ROWS)], slot_ref.at[t], sem_probe.at[t])
        )
        probes[t].start()
        fetch(second_ref, t, right_ref, sem_right)
    for t in range(NT):
        fetch(first_ref, t, left_ref, sem_left)
    for t in range(NT):
        probes[t].wait()
        arrived(t, right_ref, sem_right)
        o_ref[t] = nt_dot(slot_ref[t], right_ref[t]).astype(BF16)
    for t in range(NT):
        arrived(t, left_ref, sem_left)


def core_products(total, cores_ref):
    parts = []
    for k in range(PANELS):
        block = total[:, k * RANK:(k + 1) * RANK]
        parts.append(nt_dot(block, cores_ref[k], HIGHEST))
    return parts


def first_kernel(part_ref, cores_ref, o_ref):
    total = part_ref[0].astype(F32)
    for q in range(1, NZ):
        total = total + part_ref[q].astype(F32)
    parts = core_products(total, cores_ref)
    for k in range(PANELS):
        half = parts[k].astype(BF16)
        for q in range(NZ):
            o_ref[q, :, k * RANK:(k + 1) * RANK] = half


def sample_kernel(core_ref, f_ref, o_ref):
    for t in range(NT):
        o_ref[t] = nn_dot(core_ref[t], f_ref[t]).astype(BF16)


def pack_gram(gram):
    row = lax.broadcasted_iota(jnp.int32, (RANK, RANK), 0)
    col = lax.broadcasted_iota(jnp.int32, (RANK, RANK), 1)
    one, two, three = (part.astype(F32) for part in split3(gram))
    diag = jnp.sum(jnp.where(row == col, two, 0.0), axis=1, keepdims=True)
    last = jnp.sum(jnp.where((row == RANK - 1) & (col == RANK - 1), two, 0.0), axis=(0, 1), keepdims=True)
    upper = jnp.where(col == row + 1, diag, 0.0)
    upper = jnp.where((row == 0) & (col == RANK - 1), last, upper)
    return jnp.where(col <= row, one, jnp.transpose(two)), jnp.where(col <= row, three, upper)


def unpack_gram(left, right):
    row = lax.broadcasted_iota(jnp.int32, (RANK, RANK), 0)
    col = lax.broadcasted_iota(jnp.int32, (RANK, RANK), 1)
    corner = (row == 0) & (col == RANK - 1)
    last = jnp.sum(jnp.where(corner, right, 0.0), axis=(0, 1), keepdims=True)
    diag = jnp.sum(jnp.where(col == row + 1, right, 0.0), axis=1, keepdims=True)
    two_diag = jnp.where((row == col) & (row < RANK - 1), diag, 0.0)
    two_diag = jnp.where((row == RANK - 1) & (col == RANK - 1), last, two_diag)
    lower = col <= row
    one = jnp.where(lower, left, 0.0)
    three = jnp.where(lower, right, 0.0)
    two = jnp.where(col > row, left, 0.0)
    strict = jnp.where(col < row, one, 0.0) + jnp.where(col < row, three, 0.0)
    full_diag = jnp.where(row == col, one + (three + two_diag), 0.0)
    below = strict + jnp.where(col < row, jnp.transpose(two), 0.0)
    return below + full_diag + jnp.transpose(below)


def fold(x):
    return jnp.concatenate([x[EXTRA * b:EXTRA * (b + 1)] for b in range(4)], axis=1)


def unfold(x):
    return jnp.concatenate([x[:, 128 * b:128 * (b + 1)] for b in range(4)], axis=0)


def gram_kernel(own_ref, other_ref, f_ref, o_ref):
    for t in range(NT):
        total = own_ref[t].astype(F32) + other_ref[t].astype(F32)
        gram = nt_dot(total, total, HIGHEST)
        hi = total.astype(BF16)
        low = (total - hi.astype(F32)).astype(BF16)
        both = nt_dot(jnp.concatenate([hi, low], axis=0), f_ref[t])
        o_ref[t, 0:RANK] = (both[0:RANK] + both[RANK:2 * RANK]).astype(BF16)
        left, right = pack_gram(gram)
        o_ref[t, RANK:RANK + EXTRA] = fold(jnp.concatenate([left, right], axis=1).astype(BF16))


def inverse_factor(gram):
    row_id = lax.broadcasted_iota(jnp.int32, (RANK, RANK), 0)
    col_id = lax.broadcasted_iota(jnp.int32, (RANK, RANK), 1)
    unit = jnp.where(row_id == col_id, 1.0, 0.0).astype(F32)
    work = jnp.concatenate([gram, unit], axis=1)
    blocks = [work[8 * b:8 * b + 8, :] for b in range(RANK // 8)]
    sub = lax.broadcasted_iota(jnp.int32, (8, 2 * RANK), 0)
    scales = []
    for p in range(RANK):
        home, at = divmod(p, 8)
        row = blocks[home][at:at + 1, :]
        pivot = row[:, p:p + 1]
        scaled = row * (1.0 / pivot)
        for b in range(home, RANK // 8):
            col = jnp.broadcast_to(blocks[b][:, p:p + 1], (8, 2 * RANK))
            if b == home:
                col = jnp.where(sub > at, col, 0.0)
            blocks[b] = blocks[b] - col * scaled
    work = jnp.concatenate(blocks, axis=0)
    diag = jnp.sum(jnp.where(row_id == col_id, work[:, 0:RANK], 0.0), axis=1, keepdims=True)
    return work[:, RANK:2 * RANK] * (1.0 / jnp.sqrt(diag))


def second_kernel(part_ref, cores_ref, o_ref):
    summed = part_ref[0].astype(F32)
    for q in range(1, NZ):
        summed = summed + part_ref[q].astype(F32)
    total = summed[0:RANK]
    packed = unfold(summed[RANK:RANK + EXTRA])
    gram = unpack_gram(packed[:, 0:RANK], packed[:, RANK:2 * RANK])
    inverse = inverse_factor(gram)
    projected = nn_dot(inverse, total, HIGHEST)
    parts = core_products(projected, cores_ref)
    one, two, _ = split3(inverse)
    extra = fold(jnp.concatenate([one, two], axis=1))
    for q in range(NZ):
        for k in range(PANELS):
            o_ref[q, 0:RANK, k * RANK:(k + 1) * RANK] = parts[k].astype(BF16)
        o_ref[q, RANK:RANK + EXTRA] = extra


def final_kernel(side_ref, core_ref, own_ref, other_ref, f_ref, basis_ref, keep_ref, send_ref):
    upper = side_ref[0] == 1
    for t in range(NT):
        extra = unfold(core_ref[t, RANK:RANK + EXTRA]).astype(F32)
        inverse = extra[:, 0:RANK] + extra[:, RANK:2 * RANK]
        total = own_ref[t].astype(F32) + other_ref[t].astype(F32)
        half = jnp.where(upper, total[:, HALF:ROWS], total[:, 0:HALF])
        basis_ref[t] = nn_dot(inverse, half, HIGHEST) * math.sqrt(2048.0)
        part = nn_dot(core_ref[t, 0:RANK], f_ref[t])
        first, last = part[:, 0:HALF], part[:, HALF:ROWS]
        keep_ref[t] = jnp.where(upper, last, first)
        send_ref[t] = jnp.where(upper, first, last).astype(BF16)


def local(factors, cores, tile_list, probes):
    swap = [(0, 1), (1, 0)]
    z = lax.axis_index("z").astype(jnp.int32).reshape(1)
    side = lax.axis_index("core").astype(jnp.int32).reshape(1)
    row_first = tile_list[:, 0].astype(jnp.int32)
    row_second = tile_list[:, 1].astype(jnp.int32)
    params = pltpu.CompilerParams(vmem_limit_bytes=32 * 1024 * 1024)

    smem = pl.BlockSpec(memory_space=pltpu.SMEM)
    hbm = pl.BlockSpec(memory_space=pl.ANY)
    vmem = pl.BlockSpec(memory_space=pltpu.VMEM)

    def call(kernel, out_shape, in_specs, *args, scratch=()):
        return pl.pallas_call(
            kernel,
            out_shape=out_shape,
            in_specs=in_specs,
            out_specs=jax.tree.map(lambda _: vmem, out_shape),
            scratch_shapes=scratch,
            compiler_params=params,
        )(*args)

    def shape(*dims, dtype=BF16):
        return jax.ShapeDtypeStruct(dims, dtype)

    def exchange(x):
        return lax.all_to_all(x, "z", 0, 0, tiled=True)

    mine = jnp.transpose(factors[0, 0], (1, 0))
    sliced = call(
        slice_kernel,
        shape(NZ, RANK, ROWS + 2 * RANK),
        [hbm, vmem],
        in_hbm(mine),
        cores[0],
        scratch=[pltpu.SemaphoreType.DMA((NZ,))],
    )
    panels = exchange(sliced)
    pieces = panels[:, :, ROWS:ROWS + 2 * RANK].astype(F32)
    all_cores = pieces[:, :, 0:RANK] + pieces[:, :, RANK:2 * RANK]
    bundles = spread(panels[:, :, 0:ROWS].reshape(DEPTH, ROWS))
    probe = in_hbm(jnp.transpose(probes, (1, 2, 0)))
    block = shape(NT, DEPTH, ROWS)
    sketch, left, right = call(
        sketch_kernel,
        (shape(NT, RANK, DEPTH), block, block),
        [smem, smem, smem] + [hbm] * (1 + BUNDLES),
        jnp.stack(locate(row_first)),
        jnp.stack(locate(row_second)),
        z,
        probe,
        *(in_hbm(bundle) for bundle in bundles),
        scratch=[pltpu.VMEM((NT, RANK, ROWS), BF16)] + [pltpu.SemaphoreType.DMA((NT,))] * 3,
    )
    first = call(first_kernel, shape(NZ, RANK, DEPTH), [vmem] * 2, exchange(sketch), all_cores)
    own = call(sample_kernel, shape(NT, RANK, ROWS), [vmem] * 2, exchange(first), left)
    other = lax.ppermute(own, "core", swap)
    tall = (NT, RANK + EXTRA, DEPTH)
    stacked = call(gram_kernel, shape(*tall), [vmem] * 3, own, other, left)
    second = call(second_kernel, shape(*tall), [vmem] * 2, exchange(stacked), all_cores)
    half = (NT, RANK, HALF)
    basis, keep, send = call(
        final_kernel,
        (shape(*half, dtype=F32), shape(*half, dtype=F32), shape(*half)),
        [smem] + [vmem] * 4,
        side,
        exchange(second),
        own,
        other,
        right,
    )
    update = keep + lax.ppermute(send, "core", swap).astype(F32)
    return jnp.transpose(basis, (2, 0, 1)), jnp.transpose(update, (2, 0, 1))


def solution(mesh):
    fine = Mesh(mesh.devices.reshape(8, 2, 4, 8), ("z", "core", "x", "y"))
    layer, col = ("z", "core"), ("x", "y")
    placed = (
        P(layer, col, None, None),
        P(layer, None, None),
        P(col, None),
        P(None, col, None),
    )
    return jax.shard_map(
        local,
        mesh=fine,
        in_specs=placed,
        out_specs=(P(layer, col, None), P(layer, col, None)),
        check_vma=False,
    )
```

```python
import math

import jax
import jax.numpy as jnp
from jax import lax
from jax.experimental import pallas as pl
from jax.experimental.pallas import tpu as pltpu
from jax.sharding import Mesh, PartitionSpec as P


F32 = jnp.float32
BF16 = jnp.bfloat16
HIGHEST = lax.Precision.HIGHEST

NZ = 8
NT = 8
RANK = 64
PANELS = 8
DEPTH = PANELS * RANK
ROWS = 256
HALF = 128
BUNDLES = 18
EXTRA = 16


def nt_dot(a, b, precision=None):
    return lax.dot_general(
        a, b, (((1,), (1,)), ((), ())), precision=precision, preferred_element_type=F32
    )


def nn_dot(a, b, precision=None):
    return lax.dot_general(
        a, b, (((1,), (0,)), ((), ())), precision=precision, preferred_element_type=F32
    )


def split3(x):
    hi = x.astype(BF16)
    rest = x - hi.astype(F32)
    mid = rest.astype(BF16)
    low = (rest - mid.astype(F32)).astype(BF16)
    return hi, mid, low


def slice_kernel(f_ref, cores_ref, o_ref, sem):
    copies = []
    for q in range(NZ):
        copies.append(
            pltpu.make_async_copy(
                f_ref.at[:, q * ROWS:(q + 1) * ROWS], o_ref.at[q, :, 0:ROWS], sem.at[q]
            )
        )
        copies[q].start()
    one, two, _ = split3(cores_ref[...])
    both = jnp.concatenate([one, two], axis=1)
    for q in range(NZ):
        o_ref[q, :, ROWS:ROWS + 2 * RANK] = both
    for copy in copies:
        copy.wait()


def in_hbm(x):
    return pltpu.with_memory_space_constraint(x, pltpu.HBM)


def either_kernel(side_ref, low_ref, high_ref, o_ref, sem):
    @pl.when(side_ref[0] == 0)
    def _():
        pltpu.make_async_copy(low_ref, o_ref, sem).start()

    @pl.when(side_ref[0] != 0)
    def _():
        pltpu.make_async_copy(high_ref, o_ref, sem).start()

    pltpu.make_async_copy(low_ref, o_ref, sem).wait()


def either(low, high):
    side = lax.axis_index("core").astype(jnp.int32).reshape(1)
    anywhere = pl.BlockSpec(memory_space=pl.ANY)
    return pl.pallas_call(
        either_kernel,
        out_shape=jax.ShapeDtypeStruct(low.shape, low.dtype),
        in_specs=[pl.BlockSpec(memory_space=pltpu.SMEM), anywhere, anywhere],
        out_specs=anywhere,
        scratch_shapes=[pltpu.SemaphoreType.DMA(())],
    )(side, low, high)


def spread(own):
    def send(value, x_step, y_step):
        pairs = []
        for x in range(4):
            for y in range(8):
                if x_step is not None:
                    pairs.append((x * 8 + y, (x + x_step) % 4 * 8 + y))
                pairs.append((32 + x * 8 + y, 32 + x * 8 + (y + y_step) % 8))
        return lax.ppermute(value, ("core", "x", "y"), pairs)

    def bundle_send(value, y_step, x_step):
        pairs = []
        for x in range(4):
            for y in range(8):
                pairs.append((x * 8 + y, x * 8 + (y + y_step) % 8))
                if x_step is not None:
                    pairs.append((32 + x * 8 + y, 32 + (x + x_step) % 4 * 8 + y))
        return lax.ppermute(value, ("core", "x", "y"), pairs)

    up1 = send(own, 1, 1)
    down1 = send(own, -1, -1)
    up2 = send(up1, 1, 1)
    down2 = send(down1, None, -1)
    up3 = send(up2, None, 1)
    down3 = send(down2, None, -1)
    up4 = send(up3, None, 1)
    near = [jnp.stack([own, up1]), jnp.stack([down1, up2])]
    far = [jnp.stack([down2, up3]), jnp.stack([down3, up4])]
    out1, out2, out3, out4, out5, out6 = ([None, None] for _ in range(6))
    for h in range(2):
        out1[h] = bundle_send(near[h], 1, 1)
        out2[h] = bundle_send(near[h], -1, -1)
    for h in range(2):
        out3[h] = bundle_send(out1[h], 1, 1)
        out4[h] = bundle_send(either(out2[h], far[h]), -1, -1)
    for h in range(2):
        out5[h] = bundle_send(either(out3[h], far[h]), 1, 1)
        out6[h] = bundle_send(out4[h], -1, -1)
    out7 = bundle_send(out3[0], 2, None)
    out8 = bundle_send(out4[1], -2, None)
    return (*near, *far, *out1, *out2, *out3, *out4, *out5, *out6, out7, out8)


def pick(index, *values):
    out = jnp.full_like(index, values[0])
    for number, value in enumerate(values[1:], 1):
        out = jnp.where(index == number, value, out)
    return out


def locate(rows):
    dx = (lax.axis_index("x").astype(jnp.int32) - rows // 8) % 4
    dy = (lax.axis_index("y").astype(jnp.int32) - rows % 8) % 8
    lower = lax.axis_index("core") == 0
    place0 = pick(dx, 0, 1, 3, 2)
    half0 = place0 // 2
    which0 = pick(dy, 0, 4, 8, 12, 16, 14, 10, 6) + half0
    place1 = pick(dy, 0, 1, 3, 1, 3, 2, 0, 2)
    half1 = place1 // 2
    which1 = jnp.where((dy <= 2) | (dy == 7), pick(dx, 0, 4, 8, 6), pick(dx, 2, 12, 14, 10)) + half1
    return jnp.where(lower, which0, which1), jnp.where(lower, place0 - 2 * half0, place1 - 2 * half1)


def sketch_kernel(first_ref, second_ref, z_ref, probe_ref, *refs):
    bundles, refs = refs[0:BUNDLES], refs[BUNDLES:]
    o_ref, left_ref, right_ref, slot_ref, sem_right, sem_left, sem_probe = refs
    start = pl.multiple_of(z_ref[0] * ROWS, ROWS)

    def fetch(place_ref, t, out_ref, sem):
        which, at = place_ref[0, t], place_ref[1, t]

        def choose(low, high):
            if high - low == 1:
                pltpu.make_async_copy(bundles[low].at[at], out_ref.at[t], sem.at[t]).start()
                return
            middle = (low + high) // 2

            @pl.when(which < middle)
            def _():
                choose(low, middle)

            @pl.when(which >= middle)
            def _():
                choose(middle, high)

        choose(0, BUNDLES)

    def arrived(t, out_ref, sem):
        pltpu.make_async_copy(bundles[0].at[0], out_ref.at[t], sem.at[t]).wait()

    probes = []
    for t in range(NT):
        probes.append(
            pltpu.make_async_copy(probe_ref.at[t, :, pl.ds(start, ROWS)], slot_ref.at[t], sem_probe.at[t])
        )
        probes[t].start()
        fetch(second_ref, t, right_ref, sem_right)
    for t in range(NT):
        fetch(first_ref, t, left_ref, sem_left)
    for t in range(NT):
        probes[t].wait()
        arrived(t, right_ref, sem_right)
        o_ref[t] = nt_dot(slot_ref[t], right_ref[t]).astype(BF16)
    for t in range(NT):
        arrived(t, left_ref, sem_left)


def core_products(total, cores_ref):
    parts = []
    for k in range(PANELS):
        block = total[:, k * RANK:(k + 1) * RANK]
        parts.append(nt_dot(block, cores_ref[k], HIGHEST))
    return parts


def first_kernel(part_ref, cores_ref, o_ref):
    total = part_ref[0].astype(F32)
    for q in range(1, NZ):
        total = total + part_ref[q].astype(F32)
    parts = core_products(total, cores_ref)
    for k in range(PANELS):
        half = parts[k].astype(BF16)
        for q in range(NZ):
            o_ref[q, :, k * RANK:(k + 1) * RANK] = half


def sample_kernel(core_ref, f_ref, o_ref):
    for t in range(NT):
        o_ref[t] = nn_dot(core_ref[t], f_ref[t]).astype(BF16)


def pack_gram(gram):
    row = lax.broadcasted_iota(jnp.int32, (RANK, RANK), 0)
    col = lax.broadcasted_iota(jnp.int32, (RANK, RANK), 1)
    one, two, three = (part.astype(F32) for part in split3(gram))
    diag = jnp.sum(jnp.where(row == col, two, 0.0), axis=1, keepdims=True)
    last = jnp.sum(jnp.where((row == RANK - 1) & (col == RANK - 1), two, 0.0), axis=(0, 1), keepdims=True)
    upper = jnp.where(col == row + 1, diag, 0.0)
    upper = jnp.where((row == 0) & (col == RANK - 1), last, upper)
    return jnp.where(col <= row, one, jnp.transpose(two)), jnp.where(col <= row, three, upper)


def unpack_gram(left, right):
    row = lax.broadcasted_iota(jnp.int32, (RANK, RANK), 0)
    col = lax.broadcasted_iota(jnp.int32, (RANK, RANK), 1)
    corner = (row == 0) & (col == RANK - 1)
    last = jnp.sum(jnp.where(corner, right, 0.0), axis=(0, 1), keepdims=True)
    diag = jnp.sum(jnp.where(col == row + 1, right, 0.0), axis=1, keepdims=True)
    two_diag = jnp.where((row == col) & (row < RANK - 1), diag, 0.0)
    two_diag = jnp.where((row == RANK - 1) & (col == RANK - 1), last, two_diag)
    lower = col <= row
    one = jnp.where(lower, left, 0.0)
    three = jnp.where(lower, right, 0.0)
    two = jnp.where(col > row, left, 0.0)
    strict = jnp.where(col < row, one, 0.0) + jnp.where(col < row, three, 0.0)
    full_diag = jnp.where(row == col, one + (three + two_diag), 0.0)
    below = strict + jnp.where(col < row, jnp.transpose(two), 0.0)
    return below + full_diag + jnp.transpose(below)


def fold(x):
    return jnp.concatenate([x[EXTRA * b:EXTRA * (b + 1)] for b in range(4)], axis=1)


def unfold(x):
    return jnp.concatenate([x[:, 128 * b:128 * (b + 1)] for b in range(4)], axis=0)


def gram_kernel(own_ref, other_ref, f_ref, o_ref):
    for t in range(NT):
        total = own_ref[t].astype(F32) + other_ref[t].astype(F32)
        gram = nt_dot(total, total, HIGHEST)
        hi = total.astype(BF16)
        low = (total - hi.astype(F32)).astype(BF16)
        both = nt_dot(jnp.concatenate([hi, low], axis=0), f_ref[t])
        o_ref[t, 0:RANK] = (both[0:RANK] + both[RANK:2 * RANK]).astype(BF16)
        left, right = pack_gram(gram)
        o_ref[t, RANK:RANK + EXTRA] = fold(jnp.concatenate([left, right], axis=1).astype(BF16))


def inverse_factor(gram):
    row_id = lax.broadcasted_iota(jnp.int32, (RANK, RANK), 0)
    col_id = lax.broadcasted_iota(jnp.int32, (RANK, RANK), 1)
    unit = jnp.where(row_id == col_id, 1.0, 0.0).astype(F32)
    work = jnp.concatenate([gram, unit], axis=1)
    blocks = [work[8 * b:8 * b + 8, :] for b in range(RANK // 8)]
    sub = lax.broadcasted_iota(jnp.int32, (8, 2 * RANK), 0)
    for p in range(RANK):
        home, at = divmod(p, 8)
        row = blocks[home][at:at + 1, :]
        pivot = row[:, p:p + 1]
        scaled = row * (1.0 / pivot)
        for b in range(home, RANK // 8):
            col = jnp.broadcast_to(blocks[b][:, p:p + 1], (8, 2 * RANK))
            if b == home:
                col = jnp.where(sub > at, col, 0.0)
            blocks[b] = blocks[b] - col * scaled
    work = jnp.concatenate(blocks, axis=0)
    diag = jnp.sum(jnp.where(row_id == col_id, work[:, 0:RANK], 0.0), axis=1, keepdims=True)
    return work[:, RANK:2 * RANK] * (1.0 / jnp.sqrt(diag))


def second_kernel(part_ref, cores_ref, o_ref):
    summed = part_ref[0].astype(F32)
    for q in range(1, NZ):
        summed = summed + part_ref[q].astype(F32)
    total = summed[0:RANK]
    packed = unfold(summed[RANK:RANK + EXTRA])
    gram = unpack_gram(packed[:, 0:RANK], packed[:, RANK:2 * RANK])
    inverse = inverse_factor(gram)
    projected = nn_dot(inverse, total, HIGHEST)
    parts = core_products(projected, cores_ref)
    one, two, _ = split3(inverse)
    extra = fold(jnp.concatenate([one, two], axis=1))
    for q in range(NZ):
        for k in range(PANELS):
            o_ref[q, 0:RANK, k * RANK:(k + 1) * RANK] = parts[k].astype(BF16)
        o_ref[q, RANK:RANK + EXTRA] = extra


def final_kernel(side_ref, core_ref, own_ref, other_ref, f_ref, basis_ref, keep_ref, send_ref):
    upper = side_ref[0] == 1
    for t in range(NT):
        extra = unfold(core_ref[t, RANK:RANK + EXTRA]).astype(F32)
        inverse = extra[:, 0:RANK] + extra[:, RANK:2 * RANK]
        total = own_ref[t].astype(F32) + other_ref[t].astype(F32)
        half = jnp.where(upper, total[:, HALF:ROWS], total[:, 0:HALF])
        basis_ref[t] = nn_dot(inverse, half, HIGHEST) * math.sqrt(2048.0)
        part = nn_dot(core_ref[t, 0:RANK], f_ref[t])
        first, last = part[:, 0:HALF], part[:, HALF:ROWS]
        keep_ref[t] = jnp.where(upper, last, first)
        send_ref[t] = jnp.where(upper, first, last).astype(BF16)


def local(factors, cores, tile_list, probes):
    swap = [(0, 1), (1, 0)]
    z = lax.axis_index("z").astype(jnp.int32).reshape(1)
    side = lax.axis_index("core").astype(jnp.int32).reshape(1)
    row_first = tile_list[:, 0].astype(jnp.int32)
    row_second = tile_list[:, 1].astype(jnp.int32)
    params = pltpu.CompilerParams(vmem_limit_bytes=32 * 1024 * 1024)

    smem = pl.BlockSpec(memory_space=pltpu.SMEM)
    hbm = pl.BlockSpec(memory_space=pl.ANY)
    vmem = pl.BlockSpec(memory_space=pltpu.VMEM)

    def call(kernel, out_shape, in_specs, *args, scratch=()):
        return pl.pallas_call(
            kernel,
            out_shape=out_shape,
            in_specs=in_specs,
            out_specs=jax.tree.map(lambda _: vmem, out_shape),
            scratch_shapes=scratch,
            compiler_params=params,
        )(*args)

    def shape(*dims, dtype=BF16):
        return jax.ShapeDtypeStruct(dims, dtype)

    def exchange(x):
        return lax.all_to_all(x, "z", 0, 0, tiled=True)

    mine = jnp.transpose(factors[0, 0], (1, 0))
    sliced = call(
        slice_kernel,
        shape(NZ, RANK, ROWS + 2 * RANK),
        [hbm, vmem],
        in_hbm(mine),
        cores[0],
        scratch=[pltpu.SemaphoreType.DMA((NZ,))],
    )
    panels = exchange(sliced)
    pieces = panels[:, :, ROWS:ROWS + 2 * RANK].astype(F32)
    all_cores = pieces[:, :, 0:RANK] + pieces[:, :, RANK:2 * RANK]
    bundles = spread(panels[:, :, 0:ROWS].reshape(DEPTH, ROWS))
    probe = in_hbm(jnp.transpose(probes, (1, 2, 0)))
    block = shape(NT, DEPTH, ROWS)
    sketch, left, right = call(
        sketch_kernel,
        (shape(NT, RANK, DEPTH), block, block),
        [smem, smem, smem] + [hbm] * (1 + BUNDLES),
        jnp.stack(locate(row_first)),
        jnp.stack(locate(row_second)),
        z,
        probe,
        *(in_hbm(bundle) for bundle in bundles),
        scratch=[pltpu.VMEM((NT, RANK, ROWS), BF16)] + [pltpu.SemaphoreType.DMA((NT,))] * 3,
    )
    first = call(first_kernel, shape(NZ, RANK, DEPTH), [vmem] * 2, exchange(sketch), all_cores)
    own = call(sample_kernel, shape(NT, RANK, ROWS), [vmem] * 2, exchange(first), left)
    other = lax.ppermute(own, "core", swap)
    tall = (NT, RANK + EXTRA, DEPTH)
    stacked = call(gram_kernel, shape(*tall), [vmem] * 3, own, other, left)
    second = call(second_kernel, shape(*tall), [vmem] * 2, exchange(stacked), all_cores)
    half = (NT, RANK, HALF)
    basis, keep, send = call(
        final_kernel,
        (shape(*half, dtype=F32), shape(*half, dtype=F32), shape(*half)),
        [smem] + [vmem] * 4,
        side,
        exchange(second),
        own,
        other,
        right,
    )
    update = keep + lax.ppermute(send, "core", swap).astype(F32)
    return jnp.transpose(basis, (2, 0, 1)), jnp.transpose(update, (2, 0, 1))


def solution(mesh):
    fine = Mesh(mesh.devices.reshape(8, 2, 4, 8), ("z", "core", "x", "y"))
    layer, col = ("z", "core"), ("x", "y")
    placed = (
        P(layer, col, None, None),
        P(layer, None, None),
        P(col, None),
        P(None, col, None),
    )
    return jax.shard_map(
        local,
        mesh=fine,
        in_specs=placed,
        out_specs=(P(layer, col, None), P(layer, col, None)),
        check_vma=False,
    )
```

```python
import math

import jax
import jax.numpy as jnp
from jax import lax
from jax.experimental import pallas as pl
from jax.experimental.pallas import tpu as pltpu
from jax.sharding import Mesh, PartitionSpec as P


F32 = jnp.float32
BF16 = jnp.bfloat16
HIGHEST = lax.Precision.HIGHEST

NZ = 8
NT = 8
RANK = 64
PANELS = 8
DEPTH = PANELS * RANK
ROWS = 256
HALF = 128
BUNDLES = 10
EXTRA = 16


def nt_dot(a, b, precision=None):
    return lax.dot_general(
        a, b, (((1,), (1,)), ((), ())), precision=precision, preferred_element_type=F32
    )


def nn_dot(a, b, precision=None):
    return lax.dot_general(
        a, b, (((1,), (0,)), ((), ())), precision=precision, preferred_element_type=F32
    )


def split3(x):
    hi = x.astype(BF16)
    rest = x - hi.astype(F32)
    mid = rest.astype(BF16)
    low = (rest - mid.astype(F32)).astype(BF16)
    return hi, mid, low


def slice_kernel(f_ref, cores_ref, o_ref, sem):
    copies = []
    for q in range(NZ):
        copies.append(
            pltpu.make_async_copy(
                f_ref.at[:, q * ROWS:(q + 1) * ROWS], o_ref.at[q, :, 0:ROWS], sem.at[q]
            )
        )
        copies[q].start()
    one, two, _ = split3(cores_ref[...])
    both = jnp.concatenate([one, two], axis=1)
    for q in range(NZ):
        o_ref[q, :, ROWS:ROWS + 2 * RANK] = both
    for copy in copies:
        copy.wait()


def in_hbm(x):
    return pltpu.with_memory_space_constraint(x, pltpu.HBM)


def either_kernel(side_ref, low_ref, high_ref, o_ref):
    @pl.when(side_ref[0] == 0)
    def _():
        o_ref[...] = low_ref[...]

    @pl.when(side_ref[0] != 0)
    def _():
        o_ref[...] = high_ref[...]


def either(low, high):
    side = lax.axis_index("core").astype(jnp.int32).reshape(1)
    vmem = pl.BlockSpec(memory_space=pltpu.VMEM)
    return pl.pallas_call(
        either_kernel,
        out_shape=jax.ShapeDtypeStruct(low.shape, low.dtype),
        in_specs=[pl.BlockSpec(memory_space=pltpu.SMEM), vmem, vmem],
        out_specs=vmem,
    )(side, low, high)


def spread(own):
    def send(value, x_step, y_step):
        pairs = []
        for x in range(4):
            for y in range(8):
                if x_step is not None:
                    pairs.append((x * 8 + y, (x + x_step) % 4 * 8 + y))
                pairs.append((32 + x * 8 + y, 32 + x * 8 + (y + y_step) % 8))
        return lax.ppermute(value, ("core", "x", "y"), pairs)

    def bundle_send(value, y_step, x_step):
        pairs = []
        for x in range(4):
            for y in range(8):
                pairs.append((x * 8 + y, x * 8 + (y + y_step) % 8))
                if x_step is not None:
                    pairs.append((32 + x * 8 + y, 32 + (x + x_step) % 4 * 8 + y))
        return lax.ppermute(value, ("core", "x", "y"), pairs)

    up1 = send(own, 1, 1)
    down1 = send(own, -1, -1)
    up2 = send(up1, 1, 1)
    down2 = send(down1, None, -1)
    up3 = send(up2, None, 1)
    down3 = send(down2, None, -1)
    up4 = send(up3, None, 1)
    near = jnp.stack([own, up1, down1, up2])
    far = jnp.stack([down2, up3, down3, up4])
    out1 = bundle_send(near, 1, 1)
    out2 = bundle_send(near, -1, -1)
    out3 = bundle_send(out1, 1, 1)
    out4 = bundle_send(either(out2, far), -1, -1)
    out5 = bundle_send(either(out3, far), 1, 1)
    out6 = bundle_send(out4, -1, -1)
    out7 = bundle_send(out3[0:2], 2, None)
    out8 = bundle_send(out4[2:4], -2, None)
    return near, far, out1, out2, out3, out4, out5, out6, out7, out8


def pick(index, *values):
    out = jnp.full_like(index, values[0])
    for number, value in enumerate(values[1:], 1):
        out = jnp.where(index == number, value, out)
    return out


def locate(rows):
    dx = (lax.axis_index("x").astype(jnp.int32) - rows // 8) % 4
    dy = (lax.axis_index("y").astype(jnp.int32) - rows % 8) % 8
    lower = lax.axis_index("core") == 0
    place0 = pick(dx, 0, 1, 3, 2)
    across = (dy == 4) & (place0 >= 2)
    which0 = jnp.where(across, 9, pick(dy, 0, 2, 4, 6, 8, 7, 5, 3))
    place0 = jnp.where(across, place0 - 2, place0)
    place1 = pick(dy, 0, 1, 3, 1, 3, 2, 0, 2)
    which1 = jnp.where((dy <= 2) | (dy == 7), pick(dx, 0, 2, 4, 3), pick(dx, 1, 6, 7, 5))
    return jnp.where(lower, which0, which1), jnp.where(lower, place0, place1)


def sketch_kernel(first_ref, second_ref, z_ref, probe_ref, *refs):
    bundles, refs = refs[0:BUNDLES], refs[BUNDLES:]
    o_ref, left_ref, right_ref, slot_ref, sem_right, sem_left, sem_probe = refs
    start = pl.multiple_of(z_ref[0] * ROWS, ROWS)

    def fetch(place_ref, t, out_ref, sem):
        which, at = place_ref[0, t], place_ref[1, t]

        def choose(low, high):
            if high - low == 1:
                pltpu.make_async_copy(bundles[low].at[at], out_ref.at[t], sem.at[t]).start()
                return
            middle = (low + high) // 2

            @pl.when(which < middle)
            def _():
                choose(low, middle)

            @pl.when(which >= middle)
            def _():
                choose(middle, high)

        choose(0, BUNDLES)

    def arrived(t, out_ref, sem):
        pltpu.make_async_copy(bundles[0].at[0], out_ref.at[t], sem.at[t]).wait()

    probes = []
    for t in range(NT):
        probes.append(
            pltpu.make_async_copy(probe_ref.at[t, :, pl.ds(start, ROWS)], slot_ref.at[t], sem_probe.at[t])
        )
        probes[t].start()
        fetch(second_ref, t, right_ref, sem_right)
    for t in range(NT):
        fetch(first_ref, t, left_ref, sem_left)
    for t in range(NT):
        probes[t].wait()
        arrived(t, right_ref, sem_right)
        o_ref[t] = nt_dot(slot_ref[t], right_ref[t]).astype(BF16)
    for t in range(NT):
        arrived(t, left_ref, sem_left)


def core_products(total, cores_ref):
    parts = []
    for k in range(PANELS):
        block = total[:, k * RANK:(k + 1) * RANK]
        parts.append(nt_dot(block, cores_ref[k], HIGHEST))
    return parts


def first_kernel(part_ref, cores_ref, o_ref):
    total = part_ref[0].astype(F32)
    for q in range(1, NZ):
        total = total + part_ref[q].astype(F32)
    parts = core_products(total, cores_ref)
    for k in range(PANELS):
        half = parts[k].astype(BF16)
        for q in range(NZ):
            o_ref[q, :, k * RANK:(k + 1) * RANK] = half


def sample_kernel(core_ref, f_ref, o_ref):
    for t in range(NT):
        o_ref[t] = nn_dot(core_ref[t], f_ref[t]).astype(BF16)


def pack_gram(gram):
    row = lax.broadcasted_iota(jnp.int32, (RANK, RANK), 0)
    col = lax.broadcasted_iota(jnp.int32, (RANK, RANK), 1)
    one, two, three = (part.astype(F32) for part in split3(gram))
    diag = jnp.sum(jnp.where(row == col, two, 0.0), axis=1, keepdims=True)
    last = jnp.sum(jnp.where((row == RANK - 1) & (col == RANK - 1), two, 0.0), axis=(0, 1), keepdims=True)
    upper = jnp.where(col == row + 1, diag, 0.0)
    upper = jnp.where((row == 0) & (col == RANK - 1), last, upper)
    return jnp.where(col <= row, one, jnp.transpose(two)), jnp.where(col <= row, three, upper)


def unpack_gram(left, right):
    row = lax.broadcasted_iota(jnp.int32, (RANK, RANK), 0)
    col = lax.broadcasted_iota(jnp.int32, (RANK, RANK), 1)
    corner = (row == 0) & (col == RANK - 1)
    last = jnp.sum(jnp.where(corner, right, 0.0), axis=(0, 1), keepdims=True)
    diag = jnp.sum(jnp.where(col == row + 1, right, 0.0), axis=1, keepdims=True)
    two_diag = jnp.where((row == col) & (row < RANK - 1), diag, 0.0)
    two_diag = jnp.where((row == RANK - 1) & (col == RANK - 1), last, two_diag)
    lower = col <= row
    one = jnp.where(lower, left, 0.0)
    three = jnp.where(lower, right, 0.0)
    two = jnp.where(col > row, left, 0.0)
    strict = jnp.where(col < row, one, 0.0) + jnp.where(col < row, three, 0.0)
    full_diag = jnp.where(row == col, one + (three + two_diag), 0.0)
    below = strict + jnp.where(col < row, jnp.transpose(two), 0.0)
    return below + full_diag + jnp.transpose(below)


def fold(x):
    return jnp.concatenate([x[EXTRA * b:EXTRA * (b + 1)] for b in range(4)], axis=1)


def unfold(x):
    return jnp.concatenate([x[:, 128 * b:128 * (b + 1)] for b in range(4)], axis=0)


def gram_kernel(own_ref, other_ref, f_ref, o_ref):
    for t in range(NT):
        total = own_ref[t].astype(F32) + other_ref[t].astype(F32)
        gram = nt_dot(total, total, HIGHEST)
        hi = total.astype(BF16)
        low = (total - hi.astype(F32)).astype(BF16)
        both = nt_dot(jnp.concatenate([hi, low], axis=0), f_ref[t])
        o_ref[t, 0:RANK] = (both[0:RANK] + both[RANK:2 * RANK]).astype(BF16)
        left, right = pack_gram(gram)
        o_ref[t, RANK:RANK + EXTRA] = fold(jnp.concatenate([left, right], axis=1).astype(BF16))


def inverse_factor(gram):
    row_id = lax.broadcasted_iota(jnp.int32, (RANK, RANK), 0)
    col_id = lax.broadcasted_iota(jnp.int32, (RANK, RANK), 1)
    unit = jnp.where(row_id == col_id, 1.0, 0.0).astype(F32)
    work = jnp.concatenate([gram, unit], axis=1)
    blocks = [work[8 * b:8 * b + 8, :] for b in range(RANK // 8)]
    sub = lax.broadcasted_iota(jnp.int32, (8, 2 * RANK), 0)
    for p in range(RANK):
        home, at = divmod(p, 8)
        row = blocks[home][at:at + 1, :]
        pivot = row[:, p:p + 1]
        scaled = row * (1.0 / pivot)
        for b in range(home, RANK // 8):
            col = jnp.broadcast_to(blocks[b][:, p:p + 1], (8, 2 * RANK))
            if b == home:
                col = jnp.where(sub > at, col, 0.0)
            blocks[b] = blocks[b] - col * scaled
    work = jnp.concatenate(blocks, axis=0)
    diag = jnp.sum(jnp.where(row_id == col_id, work[:, 0:RANK], 0.0), axis=1, keepdims=True)
    return work[:, RANK:2 * RANK] * (1.0 / jnp.sqrt(diag))


def second_kernel(part_ref, cores_ref, o_ref):
    summed = part_ref[0].astype(F32)
    for q in range(1, NZ):
        summed = summed + part_ref[q].astype(F32)
    total = summed[0:RANK]
    packed = unfold(summed[RANK:RANK + EXTRA])
    gram = unpack_gram(packed[:, 0:RANK], packed[:, RANK:2 * RANK])
    inverse = inverse_factor(gram)
    projected = nn_dot(inverse, total, HIGHEST)
    parts = core_products(projected, cores_ref)
    one, two, _ = split3(inverse)
    extra = fold(jnp.concatenate([one, two], axis=1))
    for q in range(NZ):
        for k in range(PANELS):
            o_ref[q, 0:RANK, k * RANK:(k + 1) * RANK] = parts[k].astype(BF16)
        o_ref[q, RANK:RANK + EXTRA] = extra


def final_kernel(side_ref, core_ref, own_ref, other_ref, f_ref, basis_ref, keep_ref, send_ref):
    upper = side_ref[0] == 1
    for t in range(NT):
        extra = unfold(core_ref[t, RANK:RANK + EXTRA]).astype(F32)
        inverse = extra[:, 0:RANK] + extra[:, RANK:2 * RANK]
        total = own_ref[t].astype(F32) + other_ref[t].astype(F32)
        half = jnp.where(upper, total[:, HALF:ROWS], total[:, 0:HALF])
        basis_ref[t] = nn_dot(inverse, half, HIGHEST) * math.sqrt(2048.0)
        part = nn_dot(core_ref[t, 0:RANK], f_ref[t])
        first, last = part[:, 0:HALF], part[:, HALF:ROWS]
        keep_ref[t] = jnp.where(upper, last, first)
        send_ref[t] = jnp.where(upper, first, last).astype(BF16)


def local(factors, cores, tile_list, probes):
    swap = [(0, 1), (1, 0)]
    z = lax.axis_index("z").astype(jnp.int32).reshape(1)
    side = lax.axis_index("core").astype(jnp.int32).reshape(1)
    row_first = tile_list[:, 0].astype(jnp.int32)
    row_second = tile_list[:, 1].astype(jnp.int32)
    params = pltpu.CompilerParams(vmem_limit_bytes=32 * 1024 * 1024)

    smem = pl.BlockSpec(memory_space=pltpu.SMEM)
    hbm = pl.BlockSpec(memory_space=pl.ANY)
    vmem = pl.BlockSpec(memory_space=pltpu.VMEM)

    def call(kernel, out_shape, in_specs, *args, scratch=()):
        return pl.pallas_call(
            kernel,
            out_shape=out_shape,
            in_specs=in_specs,
            out_specs=jax.tree.map(lambda _: vmem, out_shape),
            scratch_shapes=scratch,
            compiler_params=params,
        )(*args)

    def shape(*dims, dtype=BF16):
        return jax.ShapeDtypeStruct(dims, dtype)

    def exchange(x):
        return lax.all_to_all(x, "z", 0, 0, tiled=True)

    mine = jnp.transpose(factors[0, 0], (1, 0))
    sliced = call(
        slice_kernel,
        shape(NZ, RANK, ROWS + 2 * RANK),
        [hbm, vmem],
        in_hbm(mine),
        cores[0],
        scratch=[pltpu.SemaphoreType.DMA((NZ,))],
    )
    panels = exchange(sliced)
    pieces = panels[:, :, ROWS:ROWS + 2 * RANK].astype(F32)
    all_cores = pieces[:, :, 0:RANK] + pieces[:, :, RANK:2 * RANK]
    bundles = spread(panels[:, :, 0:ROWS].reshape(DEPTH, ROWS))
    probe = in_hbm(jnp.transpose(probes, (1, 2, 0)))
    block = shape(NT, DEPTH, ROWS)
    sketch, left, right = call(
        sketch_kernel,
        (shape(NT, RANK, DEPTH), block, block),
        [smem, smem, smem] + [hbm] * (1 + BUNDLES),
        jnp.stack(locate(row_first)),
        jnp.stack(locate(row_second)),
        z,
        probe,
        *(in_hbm(bundle) for bundle in bundles),
        scratch=[pltpu.VMEM((NT, RANK, ROWS), BF16)] + [pltpu.SemaphoreType.DMA((NT,))] * 3,
    )
    first = call(first_kernel, shape(NZ, RANK, DEPTH), [vmem] * 2, exchange(sketch), all_cores)
    own = call(sample_kernel, shape(NT, RANK, ROWS), [vmem] * 2, exchange(first), left)
    other = lax.ppermute(own, "core", swap)
    tall = (NT, RANK + EXTRA, DEPTH)
    stacked = call(gram_kernel, shape(*tall), [vmem] * 3, own, other, left)
    second = call(second_kernel, shape(*tall), [vmem] * 2, exchange(stacked), all_cores)
    half = (NT, RANK, HALF)
    basis, keep, send = call(
        final_kernel,
        (shape(*half, dtype=F32), shape(*half, dtype=F32), shape(*half)),
        [smem] + [vmem] * 4,
        side,
        exchange(second),
        own,
        other,
        right,
    )
    update = keep + lax.ppermute(send, "core", swap).astype(F32)
    return jnp.transpose(basis, (2, 0, 1)), jnp.transpose(update, (2, 0, 1))


def solution(mesh):
    fine = Mesh(mesh.devices.reshape(8, 2, 4, 8), ("z", "core", "x", "y"))
    layer, col = ("z", "core"), ("x", "y")
    placed = (
        P(layer, col, None, None),
        P(layer, None, None),
        P(col, None),
        P(None, col, None),
    )
    return jax.shard_map(
        local,
        mesh=fine,
        in_specs=placed,
        out_specs=(P(layer, col, None), P(layer, col, None)),
        check_vma=False,
    )
```

```python
import math

import jax
import jax.numpy as jnp
from jax import lax
from jax.experimental import pallas as pl
from jax.experimental.pallas import tpu as pltpu
from jax.sharding import Mesh, PartitionSpec as P


F32 = jnp.float32
BF16 = jnp.bfloat16
HIGHEST = lax.Precision.HIGHEST

NZ = 8
NT = 8
RANK = 64
PANELS = 8
DEPTH = PANELS * RANK
ROWS = 256
HALF = 128
BUNDLES = 24
EXTRA = 16


def nt_dot(a, b, precision=None):
    return lax.dot_general(
        a, b, (((1,), (1,)), ((), ())), precision=precision, preferred_element_type=F32
    )


def nn_dot(a, b, precision=None):
    return lax.dot_general(
        a, b, (((1,), (0,)), ((), ())), precision=precision, preferred_element_type=F32
    )


def split3(x):
    hi = x.astype(BF16)
    rest = x - hi.astype(F32)
    mid = rest.astype(BF16)
    low = (rest - mid.astype(F32)).astype(BF16)
    return hi, mid, low


def slice_kernel(f_ref, cores_ref, o_ref, sem):
    copies = []
    for q in range(NZ):
        copies.append(
            pltpu.make_async_copy(
                f_ref.at[:, q * ROWS:(q + 1) * ROWS], o_ref.at[q, :, 0:ROWS], sem.at[q]
            )
        )
        copies[q].start()
    one, two, _ = split3(cores_ref[...])
    both = jnp.concatenate([one, two], axis=1)
    for q in range(NZ):
        o_ref[q, :, ROWS:ROWS + 2 * RANK] = both
    for copy in copies:
        copy.wait()


def in_hbm(x):
    return pltpu.with_memory_space_constraint(x, pltpu.HBM)


def spread(own):
    def send(value, x_step, y_step):
        pairs = []
        for x in range(4):
            for y in range(8):
                if x_step is not None:
                    pairs.append((x * 8 + y, (x + x_step) % 4 * 8 + y))
                pairs.append((32 + x * 8 + y, 32 + x * 8 + (y + y_step) % 8))
        return lax.ppermute(value, ("core", "x", "y"), pairs)

    def bundle_send(value, y_step, x_step):
        pairs = []
        for x in range(4):
            for y in range(8):
                if y_step is not None:
                    pairs.append((x * 8 + y, x * 8 + (y + y_step) % 8))
                if x_step is not None:
                    pairs.append((32 + x * 8 + y, 32 + (x + x_step) % 4 * 8 + y))
        return lax.ppermute(value, ("core", "x", "y"), pairs)

    up1 = send(own, 1, 1)
    down1 = send(own, -1, -1)
    up2 = send(up1, 1, 1)
    down2 = send(down1, None, -1)
    up3 = send(up2, None, 1)
    down3 = send(down2, None, -1)
    up4 = send(up3, None, 1)
    near = [jnp.stack([own, up1]), jnp.stack([down1, up2])]
    far = [jnp.stack([down2, up3]), jnp.stack([down3, up4])]
    out1, out2, out3, a4, b4, a5, b5, a6, b6 = ([None, None] for _ in range(9))
    for h in range(2):
        out1[h] = bundle_send(near[h], 1, 1)
        out2[h] = bundle_send(near[h], -1, -1)
        out3[h] = bundle_send(out1[h], 1, 1)
        a4[h] = bundle_send(out2[h], -1, None)
        b4[h] = bundle_send(far[h], None, -1)
        a5[h] = bundle_send(out3[h], 1, None)
        b5[h] = bundle_send(far[h], None, 1)
        a6[h] = bundle_send(a4[h], -1, None)
        b6[h] = bundle_send(b4[h], None, -1)
    out7 = bundle_send(a5[0], 1, None)
    out8 = bundle_send(a6[1], -1, None)
    return (*near, *far, *out1, *out2, *out3, *a4, *b4, *a5, *b5, *a6, *b6, out7, out8)


def pick(index, *values):
    out = jnp.full_like(index, values[0])
    for number, value in enumerate(values[1:], 1):
        out = jnp.where(index == number, value, out)
    return out


def locate(rows):
    dx = (lax.axis_index("x").astype(jnp.int32) - rows // 8) % 4
    dy = (lax.axis_index("y").astype(jnp.int32) - rows % 8) % 8
    lower = lax.axis_index("core") == 0
    place0 = pick(dx, 0, 1, 3, 2)
    half0 = place0 // 2
    which0 = pick(dy, 0, 4, 8, 14, 22, 18, 10, 6) + half0
    place1 = pick(dy, 0, 1, 3, 1, 3, 2, 0, 2)
    half1 = place1 // 2
    which1 = jnp.where((dy <= 2) | (dy == 7), pick(dx, 0, 4, 8, 6), pick(dx, 2, 16, 20, 12)) + half1
    return jnp.where(lower, which0, which1), jnp.where(lower, place0 - 2 * half0, place1 - 2 * half1)


def sketch_kernel(first_ref, second_ref, z_ref, probe_ref, *refs):
    bundles, refs = refs[0:BUNDLES], refs[BUNDLES:]
    o_ref, left_ref, right_ref, slot_ref, sem_right, sem_left, sem_probe = refs
    start = pl.multiple_of(z_ref[0] * ROWS, ROWS)

    def fetch(place_ref, t, out_ref, sem):
        which, at = place_ref[0, t], place_ref[1, t]

        def choose(low, high):
            if high - low == 1:
                pltpu.make_async_copy(bundles[low].at[at], out_ref.at[t], sem.at[t]).start()
                return
            middle = (low + high) // 2

            @pl.when(which < middle)
            def _():
                choose(low, middle)

            @pl.when(which >= middle)
            def _():
                choose(middle, high)

        choose(0, BUNDLES)

    def arrived(t, out_ref, sem):
        pltpu.make_async_copy(bundles[0].at[0], out_ref.at[t], sem.at[t]).wait()

    probes = []
    for t in range(NT):
        probes.append(
            pltpu.make_async_copy(probe_ref.at[t, :, pl.ds(start, ROWS)], slot_ref.at[t], sem_probe.at[t])
        )
        probes[t].start()
        fetch(second_ref, t, right_ref, sem_right)
    for t in range(NT):
        fetch(first_ref, t, left_ref, sem_left)
    for t in range(NT):
        probes[t].wait()
        arrived(t, right_ref, sem_right)
        o_ref[t] = nt_dot(slot_ref[t], right_ref[t]).astype(BF16)
    for t in range(NT):
        arrived(t, left_ref, sem_left)


def core_products(total, cores_ref):
    parts = []
    for k in range(PANELS):
        block = total[:, k * RANK:(k + 1) * RANK]
        parts.append(nt_dot(block, cores_ref[k], HIGHEST))
    return parts


def first_kernel(part_ref, cores_ref, o_ref):
    total = part_ref[0].astype(F32)
    for q in range(1, NZ):
        total = total + part_ref[q].astype(F32)
    parts = core_products(total, cores_ref)
    for k in range(PANELS):
        half = parts[k].astype(BF16)
        for q in range(NZ):
            o_ref[q, :, k * RANK:(k + 1) * RANK] = half


def sample_kernel(core_ref, f_ref, o_ref):
    for t in range(NT):
        o_ref[t] = nn_dot(core_ref[t], f_ref[t]).astype(BF16)


def pack_gram(gram):
    row = lax.broadcasted_iota(jnp.int32, (RANK, RANK), 0)
    col = lax.broadcasted_iota(jnp.int32, (RANK, RANK), 1)
    one, two, three = (part.astype(F32) for part in split3(gram))
    diag = jnp.sum(jnp.where(row == col, two, 0.0), axis=1, keepdims=True)
    last = jnp.sum(jnp.where((row == RANK - 1) & (col == RANK - 1), two, 0.0), axis=(0, 1), keepdims=True)
    upper = jnp.where(col == row + 1, diag, 0.0)
    upper = jnp.where((row == 0) & (col == RANK - 1), last, upper)
    return jnp.where(col <= row, one, jnp.transpose(two)), jnp.where(col <= row, three, upper)


def unpack_gram(left, right):
    row = lax.broadcasted_iota(jnp.int32, (RANK, RANK), 0)
    col = lax.broadcasted_iota(jnp.int32, (RANK, RANK), 1)
    corner = (row == 0) & (col == RANK - 1)
    last = jnp.sum(jnp.where(corner, right, 0.0), axis=(0, 1), keepdims=True)
    diag = jnp.sum(jnp.where(col == row + 1, right, 0.0), axis=1, keepdims=True)
    two_diag = jnp.where((row == col) & (row < RANK - 1), diag, 0.0)
    two_diag = jnp.where((row == RANK - 1) & (col == RANK - 1), last, two_diag)
    lower = col <= row
    one = jnp.where(lower, left, 0.0)
    three = jnp.where(lower, right, 0.0)
    two = jnp.where(col > row, left, 0.0)
    strict = jnp.where(col < row, one, 0.0) + jnp.where(col < row, three, 0.0)
    full_diag = jnp.where(row == col, one + (three + two_diag), 0.0)
    below = strict + jnp.where(col < row, jnp.transpose(two), 0.0)
    return below + full_diag + jnp.transpose(below)


def fold(x):
    return jnp.concatenate([x[EXTRA * b:EXTRA * (b + 1)] for b in range(4)], axis=1)


def unfold(x):
    return jnp.concatenate([x[:, 128 * b:128 * (b + 1)] for b in range(4)], axis=0)


def gram_kernel(own_ref, other_ref, f_ref, o_ref):
    for t in range(NT):
        total = own_ref[t].astype(F32) + other_ref[t].astype(F32)
        gram = nt_dot(total, total, HIGHEST)
        hi = total.astype(BF16)
        low = (total - hi.astype(F32)).astype(BF16)
        both = nt_dot(jnp.concatenate([hi, low], axis=0), f_ref[t])
        o_ref[t, 0:RANK] = (both[0:RANK] + both[RANK:2 * RANK]).astype(BF16)
        left, right = pack_gram(gram)
        o_ref[t, RANK:RANK + EXTRA] = fold(jnp.concatenate([left, right], axis=1).astype(BF16))


def inverse_factor(gram):
    row_id = lax.broadcasted_iota(jnp.int32, (RANK, RANK), 0)
    col_id = lax.broadcasted_iota(jnp.int32, (RANK, RANK), 1)
    unit = jnp.where(row_id == col_id, 1.0, 0.0).astype(F32)
    work = jnp.concatenate([gram, unit], axis=1)
    blocks = [work[8 * b:8 * b + 8, :] for b in range(RANK // 8)]
    sub = lax.broadcasted_iota(jnp.int32, (8, 2 * RANK), 0)
    for p in range(RANK):
        home, at = divmod(p, 8)
        row = blocks[home][at:at + 1, :]
        pivot = row[:, p:p + 1]
        scaled = row * (1.0 / pivot)
        for b in range(home, RANK // 8):
            col = jnp.broadcast_to(blocks[b][:, p:p + 1], (8, 2 * RANK))
            if b == home:
                col = jnp.where(sub > at, col, 0.0)
            blocks[b] = blocks[b] - col * scaled
    work = jnp.concatenate(blocks, axis=0)
    diag = jnp.sum(jnp.where(row_id == col_id, work[:, 0:RANK], 0.0), axis=1, keepdims=True)
    return work[:, RANK:2 * RANK] * (1.0 / jnp.sqrt(diag))


def second_kernel(part_ref, cores_ref, o_ref):
    summed = part_ref[0].astype(F32)
    for q in range(1, NZ):
        summed = summed + part_ref[q].astype(F32)
    total = summed[0:RANK]
    packed = unfold(summed[RANK:RANK + EXTRA])
    gram = unpack_gram(packed[:, 0:RANK], packed[:, RANK:2 * RANK])
    inverse = inverse_factor(gram)
    projected = nn_dot(inverse, total, HIGHEST)
    parts = core_products(projected, cores_ref)
    one, two, _ = split3(inverse)
    extra = fold(jnp.concatenate([one, two], axis=1))
    for q in range(NZ):
        for k in range(PANELS):
            o_ref[q, 0:RANK, k * RANK:(k + 1) * RANK] = parts[k].astype(BF16)
        o_ref[q, RANK:RANK + EXTRA] = extra


def final_kernel(side_ref, core_ref, own_ref, other_ref, f_ref, basis_ref, keep_ref, send_ref):
    upper = side_ref[0] == 1
    for t in range(NT):
        extra = unfold(core_ref[t, RANK:RANK + EXTRA]).astype(F32)
        inverse = extra[:, 0:RANK] + extra[:, RANK:2 * RANK]
        total = own_ref[t].astype(F32) + other_ref[t].astype(F32)
        half = jnp.where(upper, total[:, HALF:ROWS], total[:, 0:HALF])
        basis_ref[t] = nn_dot(inverse, half, HIGHEST) * math.sqrt(2048.0)
        part = nn_dot(core_ref[t, 0:RANK], f_ref[t])
        first, last = part[:, 0:HALF], part[:, HALF:ROWS]
        keep_ref[t] = jnp.where(upper, last, first)
        send_ref[t] = jnp.where(upper, first, last).astype(BF16)


def local(factors, cores, tile_list, probes):
    swap = [(0, 1), (1, 0)]
    z = lax.axis_index("z").astype(jnp.int32).reshape(1)
    side = lax.axis_index("core").astype(jnp.int32).reshape(1)
    row_first = tile_list[:, 0].astype(jnp.int32)
    row_second = tile_list[:, 1].astype(jnp.int32)
    params = pltpu.CompilerParams(vmem_limit_bytes=32 * 1024 * 1024)

    smem = pl.BlockSpec(memory_space=pltpu.SMEM)
    hbm = pl.BlockSpec(memory_space=pl.ANY)
    vmem = pl.BlockSpec(memory_space=pltpu.VMEM)

    def call(kernel, out_shape, in_specs, *args, scratch=()):
        return pl.pallas_call(
            kernel,
            out_shape=out_shape,
            in_specs=in_specs,
            out_specs=jax.tree.map(lambda _: vmem, out_shape),
            scratch_shapes=scratch,
            compiler_params=params,
        )(*args)

    def shape(*dims, dtype=BF16):
        return jax.ShapeDtypeStruct(dims, dtype)

    def exchange(x):
        return lax.all_to_all(x, "z", 0, 0, tiled=True)

    mine = jnp.transpose(factors[0, 0], (1, 0))
    sliced = call(
        slice_kernel,
        shape(NZ, RANK, ROWS + 2 * RANK),
        [hbm, vmem],
        in_hbm(mine),
        cores[0],
        scratch=[pltpu.SemaphoreType.DMA((NZ,))],
    )
    panels = exchange(sliced)
    pieces = panels[:, :, ROWS:ROWS + 2 * RANK].astype(F32)
    all_cores = pieces[:, :, 0:RANK] + pieces[:, :, RANK:2 * RANK]
    bundles = spread(panels[:, :, 0:ROWS].reshape(DEPTH, ROWS))
    probe = in_hbm(jnp.transpose(probes, (1, 2, 0)))
    block = shape(NT, DEPTH, ROWS)
    sketch, left, right = call(
        sketch_kernel,
        (shape(NT, RANK, DEPTH), block, block),
        [smem, smem, smem] + [hbm] * (1 + BUNDLES),
        jnp.stack(locate(row_first)),
        jnp.stack(locate(row_second)),
        z,
        probe,
        *(in_hbm(bundle) for bundle in bundles),
        scratch=[pltpu.VMEM((NT, RANK, ROWS), BF16)] + [pltpu.SemaphoreType.DMA((NT,))] * 3,
    )
    first = call(first_kernel, shape(NZ, RANK, DEPTH), [vmem] * 2, exchange(sketch), all_cores)
    own = call(sample_kernel, shape(NT, RANK, ROWS), [vmem] * 2, exchange(first), left)
    other = lax.ppermute(own, "core", swap)
    tall = (NT, RANK + EXTRA, DEPTH)
    stacked = call(gram_kernel, shape(*tall), [vmem] * 3, own, other, left)
    second = call(second_kernel, shape(*tall), [vmem] * 2, exchange(stacked), all_cores)
    half = (NT, RANK, HALF)
    basis, keep, send = call(
        final_kernel,
        (shape(*half, dtype=F32), shape(*half, dtype=F32), shape(*half)),
        [smem] + [vmem] * 4,
        side,
        exchange(second),
        own,
        other,
        right,
    )
    update = keep + lax.ppermute(send, "core", swap).astype(F32)
    return jnp.transpose(basis, (2, 0, 1)), jnp.transpose(update, (2, 0, 1))


def solution(mesh):
    fine = Mesh(mesh.devices.reshape(8, 2, 4, 8), ("z", "core", "x", "y"))
    layer, col = ("z", "core"), ("x", "y")
    placed = (
        P(layer, col, None, None),
        P(layer, None, None),
        P(col, None),
        P(None, col, None),
    )
    return jax.shard_map(
        local,
        mesh=fine,
        in_specs=placed,
        out_specs=(P(layer, col, None), P(layer, col, None)),
        check_vma=False,
    )
```

```python
import math

import jax
import jax.numpy as jnp
from jax import lax
from jax.experimental import pallas as pl
from jax.experimental.pallas import tpu as pltpu
from jax.sharding import Mesh, PartitionSpec as P


F32 = jnp.float32
BF16 = jnp.bfloat16
HIGHEST = lax.Precision.HIGHEST

NZ = 8
NT = 8
RANK = 64
PANELS = 8
DEPTH = PANELS * RANK
ROWS = 256
HALF = 128
BUNDLES = 18
EXTRA = 16


def nt_dot(a, b, precision=None):
    return lax.dot_general(
        a, b, (((1,), (1,)), ((), ())), precision=precision, preferred_element_type=F32
    )


def nn_dot(a, b, precision=None):
    return lax.dot_general(
        a, b, (((1,), (0,)), ((), ())), precision=precision, preferred_element_type=F32
    )


def split3(x):
    hi = x.astype(BF16)
    rest = x - hi.astype(F32)
    mid = rest.astype(BF16)
    low = (rest - mid.astype(F32)).astype(BF16)
    return hi, mid, low


def slice_kernel(f_ref, cores_ref, o_ref, sem):
    copies = []
    for q in range(NZ):
        copies.append(
            pltpu.make_async_copy(
                f_ref.at[:, q * ROWS:(q + 1) * ROWS], o_ref.at[q, :, 0:ROWS], sem.at[q]
            )
        )
        copies[q].start()
    one, two, _ = split3(cores_ref[...])
    both = jnp.concatenate([one, two], axis=1)
    for q in range(NZ):
        o_ref[q, :, ROWS:ROWS + 2 * RANK] = both
    for copy in copies:
        copy.wait()


def in_hbm(x):
    return pltpu.with_memory_space_constraint(x, pltpu.HBM)


def either_kernel(side_ref, low_ref, high_ref, o_ref):
    @pl.when(side_ref[0] == 0)
    def _():
        o_ref[...] = low_ref[...]

    @pl.when(side_ref[0] != 0)
    def _():
        o_ref[...] = high_ref[...]


def either(low, high):
    side = lax.axis_index("core").astype(jnp.int32).reshape(1)
    vmem = pl.BlockSpec(memory_space=pltpu.VMEM)
    return pl.pallas_call(
        either_kernel,
        out_shape=jax.ShapeDtypeStruct(low.shape, low.dtype),
        in_specs=[pl.BlockSpec(memory_space=pltpu.SMEM), vmem, vmem],
        out_specs=vmem,
    )(side, low, high)


def spread(own):
    def send(value, x_step, y_step):
        pairs = []
        for x in range(4):
            for y in range(8):
                if x_step is not None:
                    pairs.append((x * 8 + y, (x + x_step) % 4 * 8 + y))
                pairs.append((32 + x * 8 + y, 32 + x * 8 + (y + y_step) % 8))
        return lax.ppermute(value, ("core", "x", "y"), pairs)

    def bundle_send(value, y_step, x_step):
        pairs = []
        for x in range(4):
            for y in range(8):
                if y_step is not None:
                    pairs.append((x * 8 + y, x * 8 + (y + y_step) % 8))
                if x_step is not None:
                    pairs.append((32 + x * 8 + y, 32 + (x + x_step) % 4 * 8 + y))
        return lax.ppermute(value, ("core", "x", "y"), pairs)

    up1 = send(own, 1, 1)
    down1 = send(own, -1, -1)
    up2 = send(up1, 1, 1)
    down2 = send(down1, None, -1)
    up3 = send(up2, None, 1)
    down3 = send(down2, None, -1)
    up4 = send(up3, None, 1)
    near = [jnp.stack([own, up1]), jnp.stack([down1, up2])]
    far = [jnp.stack([down2, up3]), jnp.stack([down3, up4])]
    out1, out2, out3, out4, out5, out6 = ([None, None] for _ in range(6))
    for h in range(2):
        out1[h] = bundle_send(near[h], 1, 1)
        out2[h] = bundle_send(either(near[h], far[h]), -1, -1)
        out3[h] = bundle_send(out1[h], 1, 1)
        out4[h] = bundle_send(out2[h], -1, -1)
        out5[h] = bundle_send(out3[h], 1, 1)
        out6[h] = bundle_send(out4[h], -1, -1)
    out7 = bundle_send(out5[1], 1, None)
    out8 = bundle_send(out6[0], -1, None)
    return (*near, *far, *out1, *out2, *out3, *out4, *out5, *out6, out8, out7)


def pick(index, *values):
    out = jnp.full_like(index, values[0])
    for number, value in enumerate(values[1:], 1):
        out = jnp.where(index == number, value, out)
    return out


def locate(rows):
    dx = (lax.axis_index("x").astype(jnp.int32) - rows // 8) % 4
    dy = (lax.axis_index("y").astype(jnp.int32) - rows % 8) % 8
    lower = lax.axis_index("core") == 0
    place0 = pick(dx, 0, 1, 3, 2)
    half0 = place0 // 2
    which0 = pick(dy, 0, 4, 8, 12, 16, 14, 10, 6) + half0
    place1 = pick(dy, 0, 1, 3, 1, 3, 2, 0, 2)
    half1 = place1 // 2
    which1 = jnp.where((dy <= 2) | (dy == 7), pick(dx, 0, 4, 8, 12), pick(dx, 2, 14, 10, 6)) + half1
    return jnp.where(lower, which0, which1), jnp.where(lower, place0 - 2 * half0, place1 - 2 * half1)


def sketch_kernel(first_ref, second_ref, z_ref, probe_ref, *refs):
    bundles, refs = refs[0:BUNDLES], refs[BUNDLES:]
    o_ref, left_ref, right_ref, slot_ref, sem_right, sem_left, sem_probe = refs
    start = pl.multiple_of(z_ref[0] * ROWS, ROWS)

    def fetch(place_ref, t, out_ref, sem):
        which, at = place_ref[0, t], place_ref[1, t]

        def choose(low, high):
            if high - low == 1:
                pltpu.make_async_copy(bundles[low].at[at], out_ref.at[t], sem.at[t]).start()
                return
            middle = (low + high) // 2

            @pl.when(which < middle)
            def _():
                choose(low, middle)

            @pl.when(which >= middle)
            def _():
                choose(middle, high)

        choose(0, BUNDLES)

    def arrived(t, out_ref, sem):
        pltpu.make_async_copy(bundles[0].at[0], out_ref.at[t], sem.at[t]).wait()

    probes = []
    for t in range(NT):
        probes.append(
            pltpu.make_async_copy(probe_ref.at[t, :, pl.ds(start, ROWS)], slot_ref.at[t], sem_probe.at[t])
        )
        probes[t].start()
        fetch(second_ref, t, right_ref, sem_right)
    for t in range(NT):
        fetch(first_ref, t, left_ref, sem_left)
    for t in range(NT):
        probes[t].wait()
        arrived(t, right_ref, sem_right)
        o_ref[t] = nt_dot(slot_ref[t], right_ref[t]).astype(BF16)
    for t in range(NT):
        arrived(t, left_ref, sem_left)


def core_products(total, cores_ref):
    parts = []
    for k in range(PANELS):
        block = total[:, k * RANK:(k + 1) * RANK]
        parts.append(nt_dot(block, cores_ref[k], HIGHEST))
    return parts


def first_kernel(part_ref, cores_ref, o_ref):
    total = part_ref[0].astype(F32)
    for q in range(1, NZ):
        total = total + part_ref[q].astype(F32)
    parts = core_products(total, cores_ref)
    for k in range(PANELS):
        half = parts[k].astype(BF16)
        for q in range(NZ):
            o_ref[q, :, k * RANK:(k + 1) * RANK] = half


def sample_kernel(core_ref, f_ref, o_ref):
    for t in range(NT):
        o_ref[t] = nn_dot(core_ref[t], f_ref[t]).astype(BF16)


def pack_gram(gram):
    row = lax.broadcasted_iota(jnp.int32, (RANK, RANK), 0)
    col = lax.broadcasted_iota(jnp.int32, (RANK, RANK), 1)
    one, two, three = (part.astype(F32) for part in split3(gram))
    diag = jnp.sum(jnp.where(row == col, two, 0.0), axis=1, keepdims=True)
    last = jnp.sum(jnp.where((row == RANK - 1) & (col == RANK - 1), two, 0.0), axis=(0, 1), keepdims=True)
    upper = jnp.where(col == row + 1, diag, 0.0)
    upper = jnp.where((row == 0) & (col == RANK - 1), last, upper)
    return jnp.where(col <= row, one, jnp.transpose(two)), jnp.where(col <= row, three, upper)


def unpack_gram(left, right):
    row = lax.broadcasted_iota(jnp.int32, (RANK, RANK), 0)
    col = lax.broadcasted_iota(jnp.int32, (RANK, RANK), 1)
    corner = (row == 0) & (col == RANK - 1)
    last = jnp.sum(jnp.where(corner, right, 0.0), axis=(0, 1), keepdims=True)
    diag = jnp.sum(jnp.where(col == row + 1, right, 0.0), axis=1, keepdims=True)
    two_diag = jnp.where((row == col) & (row < RANK - 1), diag, 0.0)
    two_diag = jnp.where((row == RANK - 1) & (col == RANK - 1), last, two_diag)
    lower = col <= row
    one = jnp.where(lower, left, 0.0)
    three = jnp.where(lower, right, 0.0)
    two = jnp.where(col > row, left, 0.0)
    strict = jnp.where(col < row, one, 0.0) + jnp.where(col < row, three, 0.0)
    full_diag = jnp.where(row == col, one + (three + two_diag), 0.0)
    below = strict + jnp.where(col < row, jnp.transpose(two), 0.0)
    return below + full_diag + jnp.transpose(below)


def fold(x):
    return jnp.concatenate([x[EXTRA * b:EXTRA * (b + 1)] for b in range(4)], axis=1)


def unfold(x):
    return jnp.concatenate([x[:, 128 * b:128 * (b + 1)] for b in range(4)], axis=0)


def gram_kernel(own_ref, other_ref, f_ref, o_ref):
    for t in range(NT):
        total = own_ref[t].astype(F32) + other_ref[t].astype(F32)
        gram = nt_dot(total, total, HIGHEST)
        hi = total.astype(BF16)
        low = (total - hi.astype(F32)).astype(BF16)
        both = nt_dot(jnp.concatenate([hi, low], axis=0), f_ref[t])
        o_ref[t, 0:RANK] = (both[0:RANK] + both[RANK:2 * RANK]).astype(BF16)
        left, right = pack_gram(gram)
        o_ref[t, RANK:RANK + EXTRA] = fold(jnp.concatenate([left, right], axis=1).astype(BF16))


def inverse_factor(gram):
    row_id = lax.broadcasted_iota(jnp.int32, (RANK, RANK), 0)
    col_id = lax.broadcasted_iota(jnp.int32, (RANK, RANK), 1)
    unit = jnp.where(row_id == col_id, 1.0, 0.0).astype(F32)
    work = jnp.concatenate([gram, unit], axis=1)
    blocks = [work[8 * b:8 * b + 8, :] for b in range(RANK // 8)]
    sub = lax.broadcasted_iota(jnp.int32, (8, 2 * RANK), 0)
    for p in range(RANK):
        home, at = divmod(p, 8)
        row = blocks[home][at:at + 1, :]
        pivot = row[:, p:p + 1]
        scaled = row * (1.0 / pivot)
        for b in range(home, RANK // 8):
            col = jnp.broadcast_to(blocks[b][:, p:p + 1], (8, 2 * RANK))
            if b == home:
                col = jnp.where(sub > at, col, 0.0)
            blocks[b] = blocks[b] - col * scaled
    work = jnp.concatenate(blocks, axis=0)
    diag = jnp.sum(jnp.where(row_id == col_id, work[:, 0:RANK], 0.0), axis=1, keepdims=True)
    return work[:, RANK:2 * RANK] * (1.0 / jnp.sqrt(diag))


def second_kernel(part_ref, cores_ref, o_ref):
    summed = part_ref[0].astype(F32)
    for q in range(1, NZ):
        summed = summed + part_ref[q].astype(F32)
    total = summed[0:RANK]
    packed = unfold(summed[RANK:RANK + EXTRA])
    gram = unpack_gram(packed[:, 0:RANK], packed[:, RANK:2 * RANK])
    inverse = inverse_factor(gram)
    projected = nn_dot(inverse, total, HIGHEST)
    parts = core_products(projected, cores_ref)
    one, two, _ = split3(inverse)
    extra = fold(jnp.concatenate([one, two], axis=1))
    for q in range(NZ):
        for k in range(PANELS):
            o_ref[q, 0:RANK, k * RANK:(k + 1) * RANK] = parts[k].astype(BF16)
        o_ref[q, RANK:RANK + EXTRA] = extra


def final_kernel(side_ref, core_ref, own_ref, other_ref, f_ref, basis_ref, keep_ref, send_ref):
    upper = side_ref[0] == 1
    for t in range(NT):
        extra = unfold(core_ref[t, RANK:RANK + EXTRA]).astype(F32)
        inverse = extra[:, 0:RANK] + extra[:, RANK:2 * RANK]
        total = own_ref[t].astype(F32) + other_ref[t].astype(F32)
        half = jnp.where(upper, total[:, HALF:ROWS], total[:, 0:HALF])
        basis_ref[t] = nn_dot(inverse, half, HIGHEST) * math.sqrt(2048.0)
        part = nn_dot(core_ref[t, 0:RANK], f_ref[t])
        first, last = part[:, 0:HALF], part[:, HALF:ROWS]
        keep_ref[t] = jnp.where(upper, last, first)
        send_ref[t] = jnp.where(upper, first, last).astype(BF16)


def local(factors, cores, tile_list, probes):
    swap = [(0, 1), (1, 0)]
    z = lax.axis_index("z").astype(jnp.int32).reshape(1)
    side = lax.axis_index("core").astype(jnp.int32).reshape(1)
    row_first = tile_list[:, 0].astype(jnp.int32)
    row_second = tile_list[:, 1].astype(jnp.int32)
    params = pltpu.CompilerParams(vmem_limit_bytes=32 * 1024 * 1024)

    smem = pl.BlockSpec(memory_space=pltpu.SMEM)
    hbm = pl.BlockSpec(memory_space=pl.ANY)
    vmem = pl.BlockSpec(memory_space=pltpu.VMEM)

    def call(kernel, out_shape, in_specs, *args, scratch=()):
        return pl.pallas_call(
            kernel,
            out_shape=out_shape,
            in_specs=in_specs,
            out_specs=jax.tree.map(lambda _: vmem, out_shape),
            scratch_shapes=scratch,
            compiler_params=params,
        )(*args)

    def shape(*dims, dtype=BF16):
        return jax.ShapeDtypeStruct(dims, dtype)

    def exchange(x):
        return lax.all_to_all(x, "z", 0, 0, tiled=True)

    mine = jnp.transpose(factors[0, 0], (1, 0))
    sliced = call(
        slice_kernel,
        shape(NZ, RANK, ROWS + 2 * RANK),
        [hbm, vmem],
        in_hbm(mine),
        cores[0],
        scratch=[pltpu.SemaphoreType.DMA((NZ,))],
    )
    panels = exchange(sliced)
    pieces = panels[:, :, ROWS:ROWS + 2 * RANK].astype(F32)
    all_cores = pieces[:, :, 0:RANK] + pieces[:, :, RANK:2 * RANK]
    bundles = spread(panels[:, :, 0:ROWS].reshape(DEPTH, ROWS))
    probe = in_hbm(jnp.transpose(probes, (1, 2, 0)))
    block = shape(NT, DEPTH, ROWS)
    sketch, left, right = call(
        sketch_kernel,
        (shape(NT, RANK, DEPTH), block, block),
        [smem, smem, smem] + [hbm] * (1 + BUNDLES),
        jnp.stack(locate(row_first)),
        jnp.stack(locate(row_second)),
        z,
        probe,
        *(in_hbm(bundle) for bundle in bundles),
        scratch=[pltpu.VMEM((NT, RANK, ROWS), BF16)] + [pltpu.SemaphoreType.DMA((NT,))] * 3,
    )
    first = call(first_kernel, shape(NZ, RANK, DEPTH), [vmem] * 2, exchange(sketch), all_cores)
    own = call(sample_kernel, shape(NT, RANK, ROWS), [vmem] * 2, exchange(first), left)
    other = lax.ppermute(own, "core", swap)
    tall = (NT, RANK + EXTRA, DEPTH)
    stacked = call(gram_kernel, shape(*tall), [vmem] * 3, own, other, left)
    second = call(second_kernel, shape(*tall), [vmem] * 2, exchange(stacked), all_cores)
    half = (NT, RANK, HALF)
    basis, keep, send = call(
        final_kernel,
        (shape(*half, dtype=F32), shape(*half, dtype=F32), shape(*half)),
        [smem] + [vmem] * 4,
        side,
        exchange(second),
        own,
        other,
        right,
    )
    update = keep + lax.ppermute(send, "core", swap).astype(F32)
    return jnp.transpose(basis, (2, 0, 1)), jnp.transpose(update, (2, 0, 1))


def solution(mesh):
    fine = Mesh(mesh.devices.reshape(8, 2, 4, 8), ("z", "core", "x", "y"))
    layer, col = ("z", "core"), ("x", "y")
    placed = (
        P(layer, col, None, None),
        P(layer, None, None),
        P(col, None),
        P(None, col, None),
    )
    return jax.shard_map(
        local,
        mesh=fine,
        in_specs=placed,
        out_specs=(P(layer, col, None), P(layer, col, None)),
        check_vma=False,
    )
```

```python
import math

import jax
import jax.numpy as jnp
from jax import lax
from jax.experimental import pallas as pl
from jax.experimental.pallas import tpu as pltpu
from jax.sharding import Mesh, PartitionSpec as P


F32 = jnp.float32
BF16 = jnp.bfloat16
HIGHEST = lax.Precision.HIGHEST

NZ = 8
NT = 8
RANK = 64
PANELS = 8
DEPTH = PANELS * RANK
ROWS = 256
HALF = 128
BUNDLES = 24
EXTRA = 16


def nt_dot(a, b, precision=None):
    return lax.dot_general(
        a, b, (((1,), (1,)), ((), ())), precision=precision, preferred_element_type=F32
    )


def nn_dot(a, b, precision=None):
    return lax.dot_general(
        a, b, (((1,), (0,)), ((), ())), precision=precision, preferred_element_type=F32
    )


def split3(x):
    hi = x.astype(BF16)
    rest = x - hi.astype(F32)
    mid = rest.astype(BF16)
    low = (rest - mid.astype(F32)).astype(BF16)
    return hi, mid, low


def slice_kernel(f_ref, cores_ref, o_ref, sem):
    copies = []
    for q in range(NZ):
        copies.append(
            pltpu.make_async_copy(
                f_ref.at[:, q * ROWS:(q + 1) * ROWS], o_ref.at[q, :, 0:ROWS], sem.at[q]
            )
        )
        copies[q].start()
    one, two, _ = split3(cores_ref[...])
    both = jnp.concatenate([one, two], axis=1)
    for q in range(NZ):
        o_ref[q, :, ROWS:ROWS + 2 * RANK] = both
    for copy in copies:
        copy.wait()


def in_hbm(x):
    return pltpu.with_memory_space_constraint(x, pltpu.HBM)


def spread(own):
    def send(value, x_step, y_step):
        pairs = []
        for x in range(4):
            for y in range(8):
                if x_step is not None:
                    pairs.append((x * 8 + y, (x + x_step) % 4 * 8 + y))
                pairs.append((32 + x * 8 + y, 32 + x * 8 + (y + y_step) % 8))
        return lax.ppermute(value, ("core", "x", "y"), pairs)

    def bundle_send(value, y_step, x_step):
        pairs = []
        for x in range(4):
            for y in range(8):
                if y_step is not None:
                    pairs.append((x * 8 + y, x * 8 + (y + y_step) % 8))
                if x_step is not None:
                    pairs.append((32 + x * 8 + y, 32 + (x + x_step) % 4 * 8 + y))
        return lax.ppermute(value, ("core", "x", "y"), pairs)

    up1 = send(own, 1, 1)
    down1 = send(own, -1, -1)
    up2 = send(up1, 1, 1)
    down2 = send(down1, None, -1)
    up3 = send(up2, None, 1)
    down3 = send(down2, None, -1)
    up4 = send(up3, None, 1)
    near = [jnp.stack([own, up1]), jnp.stack([down1, up2])]
    far = [jnp.stack([down2, up3]), jnp.stack([down3, up4])]
    out1, out2, out3, a4, b4, a5, b5, a6, b6 = ([None, None] for _ in range(9))
    for h in range(2):
        out1[h] = bundle_send(near[h], 1, 1)
        out2[h] = bundle_send(near[h], -1, -1)
        out3[h] = bundle_send(out1[h], 1, 1)
        a4[h] = bundle_send(out2[h], -1, None)
        b4[h] = bundle_send(far[h], None, -1)
        a5[h] = bundle_send(out3[h], 1, None)
        b5[h] = bundle_send(far[h], None, 1)
        a6[h] = bundle_send(a4[h], -1, None)
        b6[h] = bundle_send(b4[h], None, -1)
    out7 = bundle_send(a5[1], 1, None)
    out8 = bundle_send(a6[0], -1, None)
    return (*near, *far, *out1, *out2, *out3, *a4, *b4, *a5, *b5, *a6, *b6, out8, out7)


def pick(index, *values):
    out = jnp.full_like(index, values[0])
    for number, value in enumerate(values[1:], 1):
        out = jnp.where(index == number, value, out)
    return out


def locate(rows):
    dx = (lax.axis_index("x").astype(jnp.int32) - rows // 8) % 4
    dy = (lax.axis_index("y").astype(jnp.int32) - rows % 8) % 8
    lower = lax.axis_index("core") == 0
    place0 = pick(dx, 0, 1, 3, 2)
    half0 = place0 // 2
    which0 = pick(dy, 0, 4, 8, 14, 22, 18, 10, 6) + half0
    place1 = pick(dy, 0, 1, 3, 1, 3, 2, 0, 2)
    half1 = place1 // 2
    which1 = jnp.where((dy <= 2) | (dy == 7), pick(dx, 0, 4, 8, 6), pick(dx, 2, 16, 20, 12)) + half1
    return jnp.where(lower, which0, which1), jnp.where(lower, place0 - 2 * half0, place1 - 2 * half1)


def sketch_kernel(first_ref, second_ref, z_ref, probe_ref, *refs):
    bundles, refs = refs[0:BUNDLES], refs[BUNDLES:]
    o_ref, left_ref, right_ref, slot_ref, sem_right, sem_left, sem_probe = refs
    start = pl.multiple_of(z_ref[0] * ROWS, ROWS)

    def fetch(place_ref, t, out_ref, sem):
        which, at = place_ref[0, t], place_ref[1, t]

        def choose(low, high):
            if high - low == 1:
                pltpu.make_async_copy(bundles[low].at[at], out_ref.at[t], sem.at[t]).start()
                return
            middle = (low + high) // 2

            @pl.when(which < middle)
            def _():
                choose(low, middle)

            @pl.when(which >= middle)
            def _():
                choose(middle, high)

        choose(0, BUNDLES)

    def arrived(t, out_ref, sem):
        pltpu.make_async_copy(bundles[0].at[0], out_ref.at[t], sem.at[t]).wait()

    probes = []
    for t in range(NT):
        probes.append(
            pltpu.make_async_copy(probe_ref.at[t, :, pl.ds(start, ROWS)], slot_ref.at[t], sem_probe.at[t])
        )
        probes[t].start()
        fetch(second_ref, t, right_ref, sem_right)
    for t in range(NT):
        fetch(first_ref, t, left_ref, sem_left)
    for t in range(NT):
        probes[t].wait()
        arrived(t, right_ref, sem_right)
        o_ref[t] = nt_dot(slot_ref[t], right_ref[t]).astype(BF16)
    for t in range(NT):
        arrived(t, left_ref, sem_left)


def core_products(total, cores_ref):
    parts = []
    for k in range(PANELS):
        block = total[:, k * RANK:(k + 1) * RANK]
        parts.append(nt_dot(block, cores_ref[k], HIGHEST))
    return parts


def first_kernel(part_ref, cores_ref, o_ref):
    total = part_ref[0].astype(F32)
    for q in range(1, NZ):
        total = total + part_ref[q].astype(F32)
    parts = core_products(total, cores_ref)
    for k in range(PANELS):
        half = parts[k].astype(BF16)
        for q in range(NZ):
            o_ref[q, :, k * RANK:(k + 1) * RANK] = half


def sample_kernel(core_ref, f_ref, o_ref):
    for t in range(NT):
        o_ref[t] = nn_dot(core_ref[t], f_ref[t]).astype(BF16)


def pack_gram(gram):
    row = lax.broadcasted_iota(jnp.int32, (RANK, RANK), 0)
    col = lax.broadcasted_iota(jnp.int32, (RANK, RANK), 1)
    one, two, three = (part.astype(F32) for part in split3(gram))
    diag = jnp.sum(jnp.where(row == col, two, 0.0), axis=1, keepdims=True)
    last = jnp.sum(jnp.where((row == RANK - 1) & (col == RANK - 1), two, 0.0), axis=(0, 1), keepdims=True)
    upper = jnp.where(col == row + 1, diag, 0.0)
    upper = jnp.where((row == 0) & (col == RANK - 1), last, upper)
    return jnp.where(col <= row, one, jnp.transpose(two)), jnp.where(col <= row, three, upper)


def unpack_gram(left, right):
    row = lax.broadcasted_iota(jnp.int32, (RANK, RANK), 0)
    col = lax.broadcasted_iota(jnp.int32, (RANK, RANK), 1)
    corner = (row == 0) & (col == RANK - 1)
    last = jnp.sum(jnp.where(corner, right, 0.0), axis=(0, 1), keepdims=True)
    diag = jnp.sum(jnp.where(col == row + 1, right, 0.0), axis=1, keepdims=True)
    two_diag = jnp.where((row == col) & (row < RANK - 1), diag, 0.0)
    two_diag = jnp.where((row == RANK - 1) & (col == RANK - 1), last, two_diag)
    lower = col <= row
    one = jnp.where(lower, left, 0.0)
    three = jnp.where(lower, right, 0.0)
    two = jnp.where(col > row, left, 0.0)
    strict = jnp.where(col < row, one, 0.0) + jnp.where(col < row, three, 0.0)
    full_diag = jnp.where(row == col, one + (three + two_diag), 0.0)
    below = strict + jnp.where(col < row, jnp.transpose(two), 0.0)
    return below + full_diag + jnp.transpose(below)


def fold(x):
    return jnp.concatenate([x[EXTRA * b:EXTRA * (b + 1)] for b in range(4)], axis=1)


def unfold(x):
    return jnp.concatenate([x[:, 128 * b:128 * (b + 1)] for b in range(4)], axis=0)


def gram_kernel(own_ref, other_ref, f_ref, o_ref):
    for t in range(NT):
        total = own_ref[t].astype(F32) + other_ref[t].astype(F32)
        gram = nt_dot(total, total, HIGHEST)
        hi = total.astype(BF16)
        low = (total - hi.astype(F32)).astype(BF16)
        both = nt_dot(jnp.concatenate([hi, low], axis=0), f_ref[t])
        o_ref[t, 0:RANK] = (both[0:RANK] + both[RANK:2 * RANK]).astype(BF16)
        left, right = pack_gram(gram)
        o_ref[t, RANK:RANK + EXTRA] = fold(jnp.concatenate([left, right], axis=1).astype(BF16))


def inverse_factor(gram):
    row_id = lax.broadcasted_iota(jnp.int32, (RANK, RANK), 0)
    col_id = lax.broadcasted_iota(jnp.int32, (RANK, RANK), 1)
    unit = jnp.where(row_id == col_id, 1.0, 0.0).astype(F32)
    work = jnp.concatenate([gram, unit], axis=1)
    blocks = [work[8 * b:8 * b + 8, :] for b in range(RANK // 8)]
    sub = lax.broadcasted_iota(jnp.int32, (8, 2 * RANK), 0)
    for p in range(RANK):
        home, at = divmod(p, 8)
        row = blocks[home][at:at + 1, :]
        pivot = row[:, p:p + 1]
        scaled = row * (1.0 / pivot)
        for b in range(home, RANK // 8):
            col = jnp.broadcast_to(blocks[b][:, p:p + 1], (8, 2 * RANK))
            if b == home:
                col = jnp.where(sub > at, col, 0.0)
            blocks[b] = blocks[b] - col * scaled
    work = jnp.concatenate(blocks, axis=0)
    diag = jnp.sum(jnp.where(row_id == col_id, work[:, 0:RANK], 0.0), axis=1, keepdims=True)
    return work[:, RANK:2 * RANK] * (1.0 / jnp.sqrt(diag))


def second_kernel(part_ref, cores_ref, o_ref):
    summed = part_ref[0].astype(F32)
    for q in range(1, NZ):
        summed = summed + part_ref[q].astype(F32)
    total = summed[0:RANK]
    packed = unfold(summed[RANK:RANK + EXTRA])
    gram = unpack_gram(packed[:, 0:RANK], packed[:, RANK:2 * RANK])
    inverse = inverse_factor(gram)
    projected = nn_dot(inverse, total, HIGHEST)
    parts = core_products(projected, cores_ref)
    one, two, _ = split3(inverse)
    extra = fold(jnp.concatenate([one, two], axis=1))
    for q in range(NZ):
        for k in range(PANELS):
            o_ref[q, 0:RANK, k * RANK:(k + 1) * RANK] = parts[k].astype(BF16)
        o_ref[q, RANK:RANK + EXTRA] = extra


def final_kernel(side_ref, core_ref, own_ref, other_ref, f_ref, basis_ref, keep_ref, send_ref):
    upper = side_ref[0] == 1
    for t in range(NT):
        extra = unfold(core_ref[t, RANK:RANK + EXTRA]).astype(F32)
        inverse = extra[:, 0:RANK] + extra[:, RANK:2 * RANK]
        total = own_ref[t].astype(F32) + other_ref[t].astype(F32)
        half = jnp.where(upper, total[:, HALF:ROWS], total[:, 0:HALF])
        basis_ref[t] = nn_dot(inverse, half, HIGHEST) * math.sqrt(2048.0)
        part = nn_dot(core_ref[t, 0:RANK], f_ref[t])
        first, last = part[:, 0:HALF], part[:, HALF:ROWS]
        keep_ref[t] = jnp.where(upper, last, first)
        send_ref[t] = jnp.where(upper, first, last).astype(BF16)


def local(factors, cores, tile_list, probes):
    swap = [(0, 1), (1, 0)]
    z = lax.axis_index("z").astype(jnp.int32).reshape(1)
    side = lax.axis_index("core").astype(jnp.int32).reshape(1)
    row_first = tile_list[:, 0].astype(jnp.int32)
    row_second = tile_list[:, 1].astype(jnp.int32)
    params = pltpu.CompilerParams(vmem_limit_bytes=12 * 1024 * 1024)

    smem = pl.BlockSpec(memory_space=pltpu.SMEM)
    hbm = pl.BlockSpec(memory_space=pl.ANY)
    vmem = pl.BlockSpec(memory_space=pltpu.VMEM)

    def call(kernel, out_shape, in_specs, *args, scratch=()):
        return pl.pallas_call(
            kernel,
            out_shape=out_shape,
            in_specs=in_specs,
            out_specs=jax.tree.map(lambda _: vmem, out_shape),
            scratch_shapes=scratch,
            compiler_params=params,
        )(*args)

    def shape(*dims, dtype=BF16):
        return jax.ShapeDtypeStruct(dims, dtype)

    def exchange(x):
        return lax.all_to_all(x, "z", 0, 0, tiled=True)

    mine = jnp.transpose(factors[0, 0], (1, 0))
    sliced = call(
        slice_kernel,
        shape(NZ, RANK, ROWS + 2 * RANK),
        [hbm, vmem],
        in_hbm(mine),
        cores[0],
        scratch=[pltpu.SemaphoreType.DMA((NZ,))],
    )
    panels = exchange(sliced)
    pieces = panels[:, :, ROWS:ROWS + 2 * RANK].astype(F32)
    all_cores = pieces[:, :, 0:RANK] + pieces[:, :, RANK:2 * RANK]
    bundles = spread(panels[:, :, 0:ROWS].reshape(DEPTH, ROWS))
    probe = in_hbm(jnp.transpose(probes, (1, 2, 0)))
    block = shape(NT, DEPTH, ROWS)
    sketch, left, right = call(
        sketch_kernel,
        (shape(NT, RANK, DEPTH), block, block),
        [smem, smem, smem] + [hbm] * (1 + BUNDLES),
        jnp.stack(locate(row_first)),
        jnp.stack(locate(row_second)),
        z,
        probe,
        *(in_hbm(bundle) for bundle in bundles),
        scratch=[pltpu.VMEM((NT, RANK, ROWS), BF16)] + [pltpu.SemaphoreType.DMA((NT,))] * 3,
    )
    first = call(first_kernel, shape(NZ, RANK, DEPTH), [vmem] * 2, exchange(sketch), all_cores)
    own = call(sample_kernel, shape(NT, RANK, ROWS), [vmem] * 2, exchange(first), left)
    other = lax.ppermute(own, "core", swap)
    tall = (NT, RANK + EXTRA, DEPTH)
    stacked = call(gram_kernel, shape(*tall), [vmem] * 3, own, other, left)
    second = call(second_kernel, shape(*tall), [vmem] * 2, exchange(stacked), all_cores)
    half = (NT, RANK, HALF)
    basis, keep, send = call(
        final_kernel,
        (shape(*half, dtype=F32), shape(*half, dtype=F32), shape(*half)),
        [smem] + [vmem] * 4,
        side,
        exchange(second),
        own,
        other,
        right,
    )
    update = keep + lax.ppermute(send, "core", swap).astype(F32)
    return jnp.transpose(basis, (2, 0, 1)), jnp.transpose(update, (2, 0, 1))


def solution(mesh):
    fine = Mesh(mesh.devices.reshape(8, 2, 4, 8), ("z", "core", "x", "y"))
    layer, col = ("z", "core"), ("x", "y")
    placed = (
        P(layer, col, None, None),
        P(layer, None, None),
        P(col, None),
        P(None, col, None),
    )
    return jax.shard_map(
        local,
        mesh=fine,
        in_specs=placed,
        out_specs=(P(layer, col, None), P(layer, col, None)),
        check_vma=False,
    )
```

```python
import math

import jax
import jax.numpy as jnp
from jax import lax
from jax.experimental import pallas as pl
from jax.experimental.pallas import tpu as pltpu
from jax.sharding import Mesh, PartitionSpec as P


F32 = jnp.float32
BF16 = jnp.bfloat16
HIGHEST = lax.Precision.HIGHEST

NZ = 8
NT = 8
RANK = 64
PANELS = 8
DEPTH = PANELS * RANK
ROWS = 256
HALF = 128
BUNDLES = 24
EXTRA = 16


def nt_dot(a, b, precision=None):
    return lax.dot_general(
        a, b, (((1,), (1,)), ((), ())), precision=precision, preferred_element_type=F32
    )


def nn_dot(a, b, precision=None):
    return lax.dot_general(
        a, b, (((1,), (0,)), ((), ())), precision=precision, preferred_element_type=F32
    )


def split3(x):
    hi = x.astype(BF16)
    rest = x - hi.astype(F32)
    mid = rest.astype(BF16)
    low = (rest - mid.astype(F32)).astype(BF16)
    return hi, mid, low


def slice_kernel(f_ref, cores_hbm, o_ref, cores_ref, sem):
    core = pltpu.make_async_copy(cores_hbm, cores_ref, sem.at[NZ])
    core.start()
    copies = []
    for q in range(NZ):
        copies.append(
            pltpu.make_async_copy(
                f_ref.at[:, q * ROWS:(q + 1) * ROWS], o_ref.at[q, :, 0:ROWS], sem.at[q]
            )
        )
        copies[q].start()
    core.wait()
    one, two, _ = split3(cores_ref[...])
    both = jnp.concatenate([one, two], axis=1)
    for q in range(NZ):
        o_ref[q, :, ROWS:ROWS + 2 * RANK] = both
    for copy in copies:
        copy.wait()


def in_hbm(x):
    return pltpu.with_memory_space_constraint(x, pltpu.HBM)


def spread(own):
    def send(value, x_step, y_step):
        pairs = []
        for x in range(4):
            for y in range(8):
                if x_step is not None:
                    pairs.append((x * 8 + y, (x + x_step) % 4 * 8 + y))
                pairs.append((32 + x * 8 + y, 32 + x * 8 + (y + y_step) % 8))
        return lax.ppermute(value, ("core", "x", "y"), pairs)

    def bundle_send(value, y_step, x_step):
        pairs = []
        for x in range(4):
            for y in range(8):
                if y_step is not None:
                    pairs.append((x * 8 + y, x * 8 + (y + y_step) % 8))
                if x_step is not None:
                    pairs.append((32 + x * 8 + y, 32 + (x + x_step) % 4 * 8 + y))
        return lax.ppermute(value, ("core", "x", "y"), pairs)

    up1 = send(own, 1, 1)
    down1 = send(own, -1, -1)
    up2 = send(up1, 1, 1)
    down2 = send(down1, None, -1)
    up3 = send(up2, None, 1)
    down3 = send(down2, None, -1)
    up4 = send(up3, None, 1)
    near = [jnp.stack([own, up1]), jnp.stack([down1, up2])]
    far = [jnp.stack([down2, up3]), jnp.stack([down3, up4])]
    out1, out2, out3, a4, b4, a5, b5, a6, b6 = ([None, None] for _ in range(9))
    for h in range(2):
        out1[h] = bundle_send(near[h], 1, 1)
        out2[h] = bundle_send(near[h], -1, -1)
        out3[h] = bundle_send(out1[h], 1, 1)
        a4[h] = bundle_send(out2[h], -1, None)
        b4[h] = bundle_send(far[h], None, -1)
        a5[h] = bundle_send(out3[h], 1, None)
        b5[h] = bundle_send(far[h], None, 1)
        a6[h] = bundle_send(a4[h], -1, None)
        b6[h] = bundle_send(b4[h], None, -1)
    out7 = bundle_send(a5[1], 1, None)
    out8 = bundle_send(a6[0], -1, None)
    return (*near, *far, *out1, *out2, *out3, *a4, *b4, *a5, *b5, *a6, *b6, out8, out7)


def pick(index, *values):
    out = jnp.full_like(index, values[0])
    for number, value in enumerate(values[1:], 1):
        out = jnp.where(index == number, value, out)
    return out


def locate(rows):
    dx = (lax.axis_index("x").astype(jnp.int32) - rows // 8) % 4
    dy = (lax.axis_index("y").astype(jnp.int32) - rows % 8) % 8
    lower = lax.axis_index("core") == 0
    place0 = pick(dx, 0, 1, 3, 2)
    half0 = place0 // 2
    which0 = pick(dy, 0, 4, 8, 14, 22, 18, 10, 6) + half0
    place1 = pick(dy, 0, 1, 3, 1, 3, 2, 0, 2)
    half1 = place1 // 2
    which1 = jnp.where((dy <= 2) | (dy == 7), pick(dx, 0, 4, 8, 6), pick(dx, 2, 16, 20, 12)) + half1
    return jnp.where(lower, which0, which1), jnp.where(lower, place0 - 2 * half0, place1 - 2 * half1)


def sketch_kernel(first_ref, second_ref, z_ref, probe_ref, *refs):
    bundles, refs = refs[0:BUNDLES], refs[BUNDLES:]
    o_ref, left_ref, right_ref, slot_ref, sem_right, sem_left, sem_probe = refs
    start = pl.multiple_of(z_ref[0] * ROWS, ROWS)

    def fetch(place_ref, t, out_ref, sem):
        which, at = place_ref[0, t], place_ref[1, t]

        def choose(low, high):
            if high - low == 1:
                pltpu.make_async_copy(bundles[low].at[at], out_ref.at[t], sem.at[t]).start()
                return
            middle = (low + high) // 2

            @pl.when(which < middle)
            def _():
                choose(low, middle)

            @pl.when(which >= middle)
            def _():
                choose(middle, high)

        choose(0, BUNDLES)

    def arrived(t, out_ref, sem):
        pltpu.make_async_copy(bundles[0].at[0], out_ref.at[t], sem.at[t]).wait()

    probes = []
    for t in range(NT):
        probes.append(
            pltpu.make_async_copy(probe_ref.at[t, :, pl.ds(start, ROWS)], slot_ref.at[t], sem_probe.at[t])
        )
        probes[t].start()
        fetch(second_ref, t, right_ref, sem_right)
    for t in range(NT):
        fetch(first_ref, t, left_ref, sem_left)
    for t in range(NT):
        probes[t].wait()
        arrived(t, right_ref, sem_right)
        o_ref[t] = nt_dot(slot_ref[t], right_ref[t]).astype(BF16)
    for t in range(NT):
        arrived(t, left_ref, sem_left)


def core_products(total, cores_ref):
    parts = []
    for k in range(PANELS):
        block = total[:, k * RANK:(k + 1) * RANK]
        parts.append(nt_dot(block, cores_ref[k], HIGHEST))
    return parts


def first_kernel(part_ref, cores_ref, o_ref):
    total = part_ref[0].astype(F32)
    for q in range(1, NZ):
        total = total + part_ref[q].astype(F32)
    parts = core_products(total, cores_ref)
    for k in range(PANELS):
        half = parts[k].astype(BF16)
        for q in range(NZ):
            o_ref[q, :, k * RANK:(k + 1) * RANK] = half


def sample_kernel(core_ref, f_ref, o_ref):
    for t in range(NT):
        o_ref[t] = nn_dot(core_ref[t], f_ref[t]).astype(BF16)


def pack_gram(gram):
    row = lax.broadcasted_iota(jnp.int32, (RANK, RANK), 0)
    col = lax.broadcasted_iota(jnp.int32, (RANK, RANK), 1)
    one, two, three = (part.astype(F32) for part in split3(gram))
    diag = jnp.sum(jnp.where(row == col, two, 0.0), axis=1, keepdims=True)
    last = jnp.sum(jnp.where((row == RANK - 1) & (col == RANK - 1), two, 0.0), axis=(0, 1), keepdims=True)
    upper = jnp.where(col == row + 1, diag, 0.0)
    upper = jnp.where((row == 0) & (col == RANK - 1), last, upper)
    return jnp.where(col <= row, one, jnp.transpose(two)), jnp.where(col <= row, three, upper)


def unpack_gram(left, right):
    row = lax.broadcasted_iota(jnp.int32, (RANK, RANK), 0)
    col = lax.broadcasted_iota(jnp.int32, (RANK, RANK), 1)
    corner = (row == 0) & (col == RANK - 1)
    last = jnp.sum(jnp.where(corner, right, 0.0), axis=(0, 1), keepdims=True)
    diag = jnp.sum(jnp.where(col == row + 1, right, 0.0), axis=1, keepdims=True)
    two_diag = jnp.where((row == col) & (row < RANK - 1), diag, 0.0)
    two_diag = jnp.where((row == RANK - 1) & (col == RANK - 1), last, two_diag)
    lower = col <= row
    one = jnp.where(lower, left, 0.0)
    three = jnp.where(lower, right, 0.0)
    two = jnp.where(col > row, left, 0.0)
    strict = jnp.where(col < row, one, 0.0) + jnp.where(col < row, three, 0.0)
    full_diag = jnp.where(row == col, one + (three + two_diag), 0.0)
    below = strict + jnp.where(col < row, jnp.transpose(two), 0.0)
    return below + full_diag + jnp.transpose(below)


def fold(x):
    return jnp.concatenate([x[EXTRA * b:EXTRA * (b + 1)] for b in range(4)], axis=1)


def unfold(x):
    return jnp.concatenate([x[:, 128 * b:128 * (b + 1)] for b in range(4)], axis=0)


def gram_kernel(own_ref, other_ref, f_ref, o_ref):
    for t in range(NT):
        total = own_ref[t].astype(F32) + other_ref[t].astype(F32)
        gram = nt_dot(total, total, HIGHEST)
        hi = total.astype(BF16)
        low = (total - hi.astype(F32)).astype(BF16)
        both = nt_dot(jnp.concatenate([hi, low], axis=0), f_ref[t])
        o_ref[t, 0:RANK] = (both[0:RANK] + both[RANK:2 * RANK]).astype(BF16)
        left, right = pack_gram(gram)
        o_ref[t, RANK:RANK + EXTRA] = fold(jnp.concatenate([left, right], axis=1).astype(BF16))


def inverse_factor(gram):
    row_id = lax.broadcasted_iota(jnp.int32, (RANK, RANK), 0)
    col_id = lax.broadcasted_iota(jnp.int32, (RANK, RANK), 1)
    unit = jnp.where(row_id == col_id, 1.0, 0.0).astype(F32)
    work = jnp.concatenate([gram, unit], axis=1)
    blocks = [work[8 * b:8 * b + 8, :] for b in range(RANK // 8)]
    sub = lax.broadcasted_iota(jnp.int32, (8, 2 * RANK), 0)
    for p in range(0, RANK, 2):
        home, at = divmod(p, 8)
        row0 = blocks[home][at:at + 1, :]
        row1 = blocks[home][at + 1:at + 2, :]
        top, side, low = row0[:, p:p + 1], row0[:, p + 1:p + 2], row1[:, p + 1:p + 2]
        scale = 1.0 / (top * low - side * side)
        first = (low * row0 - side * row1) * scale
        second = (top * row1 - side * row0) * scale
        inner = row1 - (side * (1.0 / top)) * row0
        for b in range(home, RANK // 8):
            col0 = jnp.broadcast_to(blocks[b][:, p:p + 1], (8, 2 * RANK))
            col1 = jnp.broadcast_to(blocks[b][:, p + 1:p + 2], (8, 2 * RANK))
            new = blocks[b] - (col0 * first + col1 * second)
            if b == home:
                new = jnp.where(sub > at + 1, new, jnp.where(sub == at + 1, inner, blocks[b]))
            blocks[b] = new
    work = jnp.concatenate(blocks, axis=0)
    diag = jnp.sum(jnp.where(row_id == col_id, work[:, 0:RANK], 0.0), axis=1, keepdims=True)
    return work[:, RANK:2 * RANK] * (1.0 / jnp.sqrt(diag))


def second_kernel(part_ref, cores_ref, o_ref):
    summed = part_ref[0].astype(F32)
    for q in range(1, NZ):
        summed = summed + part_ref[q].astype(F32)
    total = summed[0:RANK]
    packed = unfold(summed[RANK:RANK + EXTRA])
    gram = unpack_gram(packed[:, 0:RANK], packed[:, RANK:2 * RANK])
    inverse = inverse_factor(gram)
    projected = nn_dot(inverse, total, HIGHEST)
    parts = core_products(projected, cores_ref)
    one, two, _ = split3(inverse)
    extra = fold(jnp.concatenate([one, two], axis=1))
    for q in range(NZ):
        for k in range(PANELS):
            o_ref[q, 0:RANK, k * RANK:(k + 1) * RANK] = parts[k].astype(BF16)
        o_ref[q, RANK:RANK + EXTRA] = extra


def final_kernel(side_ref, core_ref, own_ref, other_ref, f_ref, basis_ref, keep_ref, send_ref):
    upper = side_ref[0] == 1
    for t in range(NT):
        extra = unfold(core_ref[t, RANK:RANK + EXTRA]).astype(F32)
        inverse = extra[:, 0:RANK] + extra[:, RANK:2 * RANK]
        total = own_ref[t].astype(F32) + other_ref[t].astype(F32)
        half = jnp.where(upper, total[:, HALF:ROWS], total[:, 0:HALF])
        basis_ref[t] = nn_dot(inverse, half, HIGHEST) * math.sqrt(2048.0)
        part = nn_dot(core_ref[t, 0:RANK], f_ref[t])
        first, last = part[:, 0:HALF], part[:, HALF:ROWS]
        keep_ref[t] = jnp.where(upper, last, first)
        send_ref[t] = jnp.where(upper, first, last).astype(BF16)


def local(factors, cores, tile_list, probes):
    swap = [(0, 1), (1, 0)]
    z = lax.axis_index("z").astype(jnp.int32).reshape(1)
    side = lax.axis_index("core").astype(jnp.int32).reshape(1)
    row_first = tile_list[:, 0].astype(jnp.int32)
    row_second = tile_list[:, 1].astype(jnp.int32)
    params = pltpu.CompilerParams(vmem_limit_bytes=32 * 1024 * 1024)

    smem = pl.BlockSpec(memory_space=pltpu.SMEM)
    hbm = pl.BlockSpec(memory_space=pl.ANY)
    vmem = pl.BlockSpec(memory_space=pltpu.VMEM)

    def call(kernel, out_shape, in_specs, *args, scratch=()):
        return pl.pallas_call(
            kernel,
            out_shape=out_shape,
            in_specs=in_specs,
            out_specs=jax.tree.map(lambda _: vmem, out_shape),
            scratch_shapes=scratch,
            compiler_params=params,
        )(*args)

    def shape(*dims, dtype=BF16):
        return jax.ShapeDtypeStruct(dims, dtype)

    def exchange(x):
        return lax.all_to_all(x, "z", 0, 0, tiled=True)

    mine = jnp.transpose(factors[0, 0], (1, 0))
    sliced = call(
        slice_kernel,
        shape(NZ, RANK, ROWS + 2 * RANK),
        [hbm, hbm],
        in_hbm(mine),
        in_hbm(cores[0]),
        scratch=[pltpu.VMEM((RANK, RANK), F32), pltpu.SemaphoreType.DMA((NZ + 1,))],
    )
    panels = exchange(sliced)
    pieces = panels[:, :, ROWS:ROWS + 2 * RANK].astype(F32)
    all_cores = pieces[:, :, 0:RANK] + pieces[:, :, RANK:2 * RANK]
    bundles = spread(panels[:, :, 0:ROWS].reshape(DEPTH, ROWS))
    probe = in_hbm(jnp.transpose(probes, (1, 2, 0)))
    block = shape(NT, DEPTH, ROWS)
    sketch, left, right = call(
        sketch_kernel,
        (shape(NT, RANK, DEPTH), block, block),
        [smem, smem, smem] + [hbm] * (1 + BUNDLES),
        jnp.stack(locate(row_first)),
        jnp.stack(locate(row_second)),
        z,
        probe,
        *(in_hbm(bundle) for bundle in bundles),
        scratch=[pltpu.VMEM((NT, RANK, ROWS), BF16)] + [pltpu.SemaphoreType.DMA((NT,))] * 3,
    )
    first = call(first_kernel, shape(NZ, RANK, DEPTH), [vmem] * 2, exchange(sketch), all_cores)
    own = call(sample_kernel, shape(NT, RANK, ROWS), [vmem] * 2, exchange(first), left)
    other = lax.ppermute(own, "core", swap)
    tall = (NT, RANK + EXTRA, DEPTH)
    stacked = call(gram_kernel, shape(*tall), [vmem] * 3, own, other, left)
    second = call(second_kernel, shape(*tall), [vmem] * 2, exchange(stacked), all_cores)
    half = (NT, RANK, HALF)
    basis, keep, send = call(
        final_kernel,
        (shape(*half, dtype=F32), shape(*half, dtype=F32), shape(*half)),
        [smem] + [vmem] * 4,
        side,
        exchange(second),
        own,
        other,
        right,
    )
    update = keep + lax.ppermute(send, "core", swap).astype(F32)
    return jnp.transpose(basis, (2, 0, 1)), jnp.transpose(update, (2, 0, 1))


def solution(mesh):
    fine = Mesh(mesh.devices.reshape(8, 2, 4, 8), ("z", "core", "x", "y"))
    layer, col = ("z", "core"), ("x", "y")
    placed = (
        P(layer, col, None, None),
        P(layer, None, None),
        P(col, None),
        P(None, col, None),
    )
    return jax.shard_map(
        local,
        mesh=fine,
        in_specs=placed,
        out_specs=(P(layer, col, None), P(layer, col, None)),
        check_vma=False,
    )
```
